128 devices in a mesh: ang: 16 (over z_hi, x, core), hgt: 8 (over z_lo, y).
Axes of the slice: x: 4, y: 4, z: 4 (z_hi: 2, z_lo: 2; z = z_hi * 2 + z_lo), core: 2. Of those that a mesh axis runs over, the one named last changes fastest.
Arguments:
- loads: float32 [4, 3, 512, 64, 128], P(None, None, 'ang', 'hgt'), may hold values from -6 to 6
- material: int32 [512, 64, 128], P('ang', 'hgt'), may hold values from 0 to 7
- support: int32 [512, 64, 128], P('ang', 'hgt'), may hold values 0 or 1
- modulus: float32 [8], replicated, may hold values from 0.5 to 5
- positions: int32 [4], replicated, may hold values from 0 to 511
Outputs:
- solution_field: float32 [4, 3, 512, 64, 128], P(None, None, 'ang', 'hgt')
- residual: float32 [4, 3, 512, 64, 128], P(None, None, 'ang', 'hgt')
The draws below stay inside these ranges and needn't reach their ends.
All inputs are finite; a program needn't handle non-finite values. No bound on the sum of `support` on one device may be relied on, other than what follows from the above.
Results may differ from the reference program's by a relative error of at most 0.0003.
Values sent between devices are 32-bit elements; how exact they have to be, the bound alone decides.
A program may use at most 64 MiB of HBM per device.

```python
import math
import jax
import jax.numpy as jnp
from jax import lax

CASES = 4
COMPS = 3
RAD = 128
NMAT = 8
ITERS = 3
CSWEEPS = 4
ANG = 512
HGT = 64
BAND = 32


def place_ends(values, rng, least, top_value):
    extent = values.shape
    spot = [jax.random.randint(jax.random.fold_in(rng, axis), (), 0, extent[axis]) for axis in range(len(extent))]
    values = values.at[tuple(spot)].set(least)
    longest = extent.index(max(extent))
    spot[longest] = (spot[longest] + 1) % extent[longest]
    return values.at[tuple(spot)].set(top_value)


def shard_levels(stream_key, dims, split, low, top_value):
    def one(axis_at, blocks):
        draws = jax.random.uniform(jax.random.fold_in(jax.random.fold_in(stream_key, 6), axis_at), (blocks,), jnp.float32, low / len(split), top_value / len(split))
        return jnp.repeat(jnp.exp(draws), dims[axis_at] // blocks).reshape((-1,) + (1,) * (len(dims) - axis_at - 1))

    factor_of = one(*split[0])
    for cut in split[1:]:
        factor_of = factor_of * one(*cut)
    return factor_of


def normal_values(own_key, extent, spread, bound, shards=(), kind=jnp.bfloat16):
    drawn = spread * jax.random.normal(own_key, extent, jnp.float32)
    if shards:
        drawn = drawn * shard_levels(own_key, extent, shards, -0.22, 0.18)
    return jnp.clip(drawn, -bound, bound).astype(kind)


def setup_inputs(seed: int = 0) -> dict:
    arg_keys = jax.random.split(jax.random.key(seed), 6)
    loads = normal_values(arg_keys[0], (CASES, COMPS, ANG, HGT, RAD), 1.0, 6.0, ((2, 16), (3, 8)), jnp.float32)
    material = place_ends(jax.random.randint(arg_keys[1], (ANG, HGT, RAD), 0, NMAT), jax.random.fold_in(arg_keys[1], 1), 0, NMAT - 1).astype(jnp.int32)
    support = place_ends((jax.random.randint(arg_keys[2], (ANG, HGT, RAD), 0, 8) < 1).astype(jnp.int32), jax.random.fold_in(arg_keys[2], 1), 0, 1)
    modulus = jnp.clip(jnp.exp(jax.random.uniform(arg_keys[3], (NMAT,), jnp.float32, math.log(0.5), math.log(5.0))), 0.5, 5.0)
    positions = place_ends(jax.random.randint(arg_keys[4], (CASES,), 0, ANG), jax.random.fold_in(arg_keys[4], 1), 0, ANG - 1).astype(jnp.int32)
    return dict(loads=loads, material=material, support=support, modulus=modulus, positions=positions)


SIGMA = 6.5
SPRING = 20.0
OMEGA = 0.8
LOAD = 3.0

def zero_pair(v, axis):
    widths = [(0, 0)] * v.ndim
    widths[axis] = (1, 1)
    padded = jnp.pad(v, widths)
    size = v.shape[axis]
    return lax.slice_in_dim(padded, 2, size + 2, axis=axis) + lax.slice_in_dim(padded, 0, size, axis=axis)

def apply_op(u, weight, spring):
    v = weight * u
    beside = jnp.roll(v, 1, axis=2) + jnp.roll(v, -1, axis=2)
    beside = beside + zero_pair(v, 3) + zero_pair(v, 4)
    return weight * (SIGMA * v - beside) + SPRING * spring * u

def coarsen(field):
    a, h, r = field.shape
    return field.reshape(a // 2, 2, h // 2, 2, r).mean(axis=(1, 3))

def restrict(r):
    c, k, a, h, n = r.shape
    return r.reshape(c, k, a // 2, 2, h // 2, 2, n).sum(axis=(3, 5)) * 0.5

def prolong(e):
    return jnp.repeat(jnp.repeat(e, 2, axis=2), 2, axis=3) * 0.5

def reference(loads, material, support, modulus, positions):
    levels = jnp.arange(NMAT, dtype=jnp.int32)
    stiff = lax.optimization_barrier(jnp.sum(jnp.where(material[None] == levels[:, None, None, None], modulus[:, None, None, None], 0.0), axis=0))
    weight = jnp.sqrt(stiff)
    spring = support.astype(jnp.float32)
    diag = SIGMA * weight * weight + SPRING * spring
    wide_c = coarsen(weight)
    spring_c = coarsen(spring)
    diag_c = SIGMA * wide_c * wide_c + SPRING * spring_c
    angles = jnp.arange(ANG, dtype=jnp.int32)
    apart = jnp.abs(angles[None, :] - positions[:, None])
    cycle_dist = jnp.minimum(apart, ANG - apart)
    hit = jnp.where(cycle_dist < BAND, -LOAD, 0.0)
    select = jnp.where(jnp.arange(COMPS, dtype=jnp.int32) == 2, 1.0, 0.0)
    right = loads + hit[:, None, :, None, None] * select[None, :, None, None, None]

    def precondition(r):
        coarse_rhs = restrict(r)
        err = OMEGA * coarse_rhs / diag_c
        for sweep in range(CSWEEPS - 1):
            err = err + OMEGA * (coarse_rhs - apply_op(err, wide_c, spring_c)) / diag_c
        return OMEGA * r / diag + prolong(err)

    def column_sum(a, b):
        return lax.optimization_barrier(jnp.sum(a * b, axis=(2, 3, 4)))[:, :, None, None, None]
    solution_field = jnp.zeros_like(right)
    residual = right
    precond = precondition(residual)
    direction = precond
    rz_now = column_sum(residual, precond)
    for step in range(ITERS):
        image = apply_op(direction, weight, spring)
        alpha = rz_now / column_sum(direction, image)
        solution_field = solution_field + alpha * direction
        residual = residual - alpha * image
        if step + 1 < ITERS:
            precond = precondition(residual)
            rz_next = column_sum(residual, precond)
            direction = precond + rz_next / rz_now * direction
            rz_now = rz_next
    return (solution_field, residual)
```

```python
import functools

import jax
import jax.numpy as jnp
from jax import lax
from jax.experimental import pallas as pl
from jax.experimental.pallas import tpu as pltpu
from jax.sharding import PartitionSpec as P

STEPS = 3
SIGMA = 6.5
SPRING = 20.0
OMEGA = 0.8
LOAD = 3.0
GROUPS = 3
MESH = pl.DeviceIdType.MESH
F32 = jnp.float32
T = (8, 128)
UP, DOWN, RIGHT, LEFT, RU, LU, RD, LD = range(8)
SHIFT = ((0, 1), (0, -1), (1, 0), (-1, 0), (1, 1), (-1, 1), (1, -1), (-1, -1))


def kernel(
    modulus, positions, loads, material, support,
    out_x, out_r,
    mat, sup, weight, spring, diag, kf, kv, iw,
    res, ys, vf, pe, co, sr, sl, sc, hl, hr, rc, pr, ring,
    fsu, fsd, fu, fd, fl, fr, tsum, pa, pb,
    in_sem, dsend, drecv, fsend, frecv, psend, precv, out_sem,
):
    na, nh = lax.axis_size("ang"), lax.axis_size("hgt")
    me_a, me_h = lax.axis_index("ang"), lax.axis_index("hgt")
    cols = loads.shape[0]
    groups = GROUPS
    per = cols // groups
    pcol = cols
    angs = 32
    sub = lax.broadcasted_iota(jnp.int32, T, 0)
    lane = lax.broadcasted_iota(jnp.int32, T, 1)
    has_up, has_down = me_h < nh - 1, me_h > 0

    def device(da, dh):
        return {"ang": lax.rem(me_a + da + na, na), "hgt": me_h + dh}

    def guarded(dh, body):
        if dh > 0:
            pl.when(has_up)(body)
        elif dh < 0:
            pl.when(has_down)(body)
        else:
            body()

    in_copies = [pltpu.make_async_copy(material, mat, in_sem.at[groups]),
                 pltpu.make_async_copy(support, sup, in_sem.at[groups + 1])]
    for copy in in_copies:
        copy.start()

    def load_copy(g):
        c = pl.ds(g * per, per)
        return pltpu.make_async_copy(loads.at[c], res.at[0, c], in_sem.at[g])

    for g in range(groups):
        load_copy(g).start()

    barrier = pltpu.get_barrier_semaphore()

    def greet_a(d, carry):
        pl.semaphore_signal(barrier, inc=1, device_id={"ang": lax.rem(me_a + d, na), "hgt": me_h}, device_id_type=MESH)
        return carry

    def greet_h(d, carry):
        pl.semaphore_signal(barrier, inc=1, device_id={"ang": me_a, "hgt": lax.rem(me_h + d, nh)}, device_id_type=MESH)
        return carry

    for da, dh in SHIFT[4:]:
        guarded(dh, lambda da=da, dh=dh: pl.semaphore_signal(
            barrier, inc=1, device_id=device(da, dh), device_id_type=MESH))
    lax.fori_loop(1, na, greet_a, 0)
    lax.fori_loop(1, nh, greet_h, 0)

    def roll(x, shift, axis=0):
        return pltpu.roll(x, shift % x.shape[axis], axis)

    def lanes(v):
        return jnp.where(lane == 0, 0.0, roll(v, 1, 1)) + jnp.where(lane == 127, 0.0, roll(v, -1, 1))

    def quad(ref, j, b, *lead):
        total = None
        for da in range(2):
            for dh in range(2):
                part = ref[(*lead, pl.ds(b * 128 + da * 8 + 2 * j + dh, 8, stride=16), slice(None))]
                total = part if total is None else total + part
        return total

    zero = jnp.zeros(T, F32)

    def clear(row, corners, fine):
        def one(c, carry):
            for k in range(STEPS):
                for j in range(3):
                    for b in range(2):
                        co[k, c, row + j, pl.ds(8 * b, 8), :] = zero
            return carry

        lax.fori_loop(0, cols + 1, one, 0)

        def two(c, carry):
            for k in range(STEPS):
                for i in range(4):
                    fine[k, c, pl.ds(8 * i, 8), :] = zero
            return carry

        lax.fori_loop(0, cols, two, 0)

        def three(c, carry):
            for k in range(STEPS):
                for d in corners:
                    rc[k, d, c] = zero
            return carry

        lax.fori_loop(0, cols // 2 + 1, three, 0)

    pl.when(jnp.logical_not(has_down))(lambda: clear(0, (RU - 4, LU - 4), fd))
    pl.when(jnp.logical_not(has_up))(lambda: clear(7, (RD - 4, LD - 4), fu))

    def deep(k, slot, first, count, d):
        c = pl.ds(first, count)
        pair = pl.ds(first // 2, (count + 1) // 2)
        if d == UP:
            src, dst = co.at[k, c, pl.ds(4, 3)], co.at[k, c, pl.ds(0, 3)]
        elif d == DOWN:
            src, dst = co.at[k, c, pl.ds(3, 3)], co.at[k, c, pl.ds(7, 3)]
        elif d == RIGHT:
            src, dst = sr.at[c], hl.at[k, c]
        elif d == LEFT:
            src, dst = sl.at[c], hr.at[k, c]
        else:
            src, dst = sc.at[d - 4, pair], rc.at[k, d - 4, pair]
        return pltpu.make_async_remote_copy(
            src_ref=src, dst_ref=dst, send_sem=dsend.at[k, slot, d], recv_sem=drecv.at[k, slot, d],
            device_id=device(*SHIFT[d]), device_id_type=MESH)

    def deep_start(k, slot, first, count):
        for d in (UP, DOWN, RU, LU, RD, LD, RIGHT, LEFT):
            guarded(SHIFT[d][1], lambda d=d: deep(k, slot, first, count, d).start())

    def deep_wait(k, slot, first, count):
        for d in range(8):
            guarded(SHIFT[d][1], lambda d=d: deep(k, slot, first, count, d).wait_send())
            guarded(-SHIFT[d][1], lambda d=d: deep(k, slot, first, count, d).wait_recv())

    def fine(k, g, d):
        c = pl.ds(g * per, per)
        if d == UP:
            src, dst = fsu.at[c], fd.at[k, c]
        elif d == DOWN:
            src, dst = fsd.at[c], fu.at[k, c]
        elif d == RIGHT:
            src, dst = vf.at[c, pl.ds(8 * (angs - 1), 8)], fl.at[k, c]
        else:
            src, dst = vf.at[c, pl.ds(0, 8)], fr.at[k, c]
        return pltpu.make_async_remote_copy(
            src_ref=src, dst_ref=dst, send_sem=fsend.at[k, g, d], recv_sem=frecv.at[k, g, d],
            device_id=device(*SHIFT[d]), device_id_type=MESH)

    def fine_start(k, g):
        for d in range(4):
            guarded(SHIFT[d][1], lambda d=d: fine(k, g, d).start())

    def fine_wait(k, g):
        for d in range(4):
            guarded(SHIFT[d][1], lambda d=d: fine(k, g, d).wait_send())
            guarded(-SHIFT[d][1], lambda d=d: fine(k, g, d).wait_recv())

    def corner_tiles(k, c):
        low = [co[k, c, 3 + h, pl.ds(0, 8), :] for h in range(4)]
        high = [co[k, c, 3 + h, pl.ds(8, 8), :] for h in range(4)]
        for t in range(2):
            sr[c, pl.ds(8 * t, 8), :] = jnp.where(sub < 4, roll(high[2 * t], 4), high[2 * t + 1])
            sl[c, pl.ds(8 * t, 8), :] = jnp.where(sub < 4, low[2 * t], roll(low[2 * t + 1], 4))
        return (
            jnp.where(sub == 5, roll(high[2], -2), high[3]),
            jnp.where(sub == 2, roll(low[2], 2), low[3]),
            jnp.where(sub == 5, roll(high[1], -2), high[0]),
            jnp.where(sub == 2, roll(low[1], 2), low[0]),
        )

    def merge(d, even, odd):
        if d in (RU, RD):
            return jnp.where(sub < 4, roll(even, 4), odd)
        return jnp.where(sub < 4, even, roll(odd, 4))

    def pack_pair(k, pair):
        even, odd = corner_tiles(k, 2 * pair), corner_tiles(k, 2 * pair + 1)
        for d in (RU, LU, RD, LD):
            sc[d - 4, pair] = merge(d, even[d - 4], odd[d - 4])

    def halo(k, c, pair, parity, h):
        if 0 <= h < 4:
            t = h // 2
            q, p = hr[k, c, pl.ds(8 * t, 8), :], hl[k, c, pl.ds(8 * t, 8), :]
            if h % 2 == 0:
                return jnp.where(sub < 4, q, roll(p, 4))
            return jnp.where(sub < 4, roll(q, 4), p)
        left = rc[k, (RU if h < 0 else RD) - 4, pair]
        right = rc[k, (LU if h < 0 else LD) - 4, pair]
        if parity == 0:
            left = roll(left, 4)
        else:
            right = roll(right, 4)
        if h in (-2, 5):
            left, right = roll(left, 2), roll(right, -2)
        return jnp.where(sub < 4, right, left)

    def ring_row(k, c, pair, parity, h):
        return [co[k, c, 3 + h, pl.ds(0, 8), :], co[k, c, 3 + h, pl.ds(8, 8), :], halo(k, c, pair, parity, h)]

    for copy in in_copies:
        copy.wait()

    def weigh(a, carry):
        rows = pl.ds(pl.multiple_of(a * 8, 8), 8)
        kind = mat[rows, :]
        stiff = zero
        for level in range(modulus.shape[0]):
            stiff = stiff + jnp.where(kind == level, modulus[level], 0.0)
        w = jnp.sqrt(stiff)
        s = sup[rows, :].astype(F32)
        d = SIGMA * w * w + SPRING * s
        weight[rows, :] = w
        spring[rows, :] = s
        diag[rows, :] = d
        kf[rows, :] = OMEGA / d
        return carry

    lax.fori_loop(0, angs, weigh, 0, unroll=4)
    for j in range(4):
        for b in range(2):
            wc = 0.25 * quad(weight, j, b)
            s = 0.25 * quad(spring, j, b)
            kd = OMEGA / (SIGMA * wc * wc + SPRING * s)
            kv[j, pl.ds(8 * b, 8), :] = 0.5 * wc * kd
            iw[j, pl.ds(8 * b, 8), :] = 0.5 / wc
            co[0, pcol, 3 + j, pl.ds(8 * b, 8), :] = wc * wc * kd
    tiles = corner_tiles(0, pcol)
    for d in (RU, LU, RD, LD):
        sc[d - 4, pcol // 2] = merge(d, tiles[d - 4], zero)

    diagonals = 2 * (has_up.astype(jnp.int32) + has_down.astype(jnp.int32))
    pl.semaphore_wait(barrier, na - 1 + nh - 1 + diagonals)
    deep_start(0, groups, pcol, 1)

    def add_moment(g, c, m, acc):
        total = jnp.sum(jnp.sum(acc, axis=0, keepdims=True), axis=1, keepdims=True)
        tsum[g] += jnp.where(jnp.logical_and(sub == m, lane == c), total, 0.0)

    def restrict(k, c):
        for j in range(4):
            for b in range(2):
                co[k, c, 3 + j, pl.ds(8 * b, 8), :] = kv[j, pl.ds(8 * b, 8), :] * quad(res, j, b, k, c)

    def send_deep(k, g):
        lax.fori_loop(0, per // 2, lambda i, carry: (pack_pair(k, g * (per // 2) + i), carry)[1], 0)
        deep_start(k, g, g * per, per)

    total_angles = na * angs

    def first(g, carry):
        load_copy(g).wait()
        tsum[g] = zero

        def column(i, carry):
            c = g * per + i
            amount = jnp.where(lax.rem(c, 3) == 2, -LOAD, 0.0)
            spot = jnp.full(T, me_a * angs, jnp.int32) - positions[c // 3]
            for a in range(angs):
                apart = jnp.abs(spot + a)
                near = jnp.minimum(apart, total_angles - apart) < angs
                res[0, c, pl.ds(8 * a, 8), :] += jnp.where(near, amount, 0.0)
            restrict(0, c)
            return carry

        lax.fori_loop(0, per, column, 0)
        send_deep(0, g)
        return carry

    lax.fori_loop(0, groups, first, 0)

    deep_wait(0, groups, pcol, 1)
    for h in range(-2, 6):
        row = ring_row(0, pcol, pcol // 2, 0, h)
        for b in range(3):
            pr[h + 2, b] = row[b]

    def sweeps(k, c, pair, parity):
        v0 = {h: ring_row(k, c, pair, parity, h) for h in range(-2, 6)}
        for h in range(-2, 6):
            for b in range(3):
                ring[0, parity, h + 2, b] = v0[h][b]
        outer = {h: [co[k, c, 3 + h, pl.ds(0, 8), :], co[k, c, 3 + h, pl.ds(8, 8), :]] for h in (-3, 6)}
        for sweep in range(3):
            def get(h, b):
                if h in outer:
                    return outer[h][b]
                return ring[sweep, parity, h + 2, b]

            for h in range(-2 + sweep, 6 - sweep):
                edge = h in (-2 + sweep, 5 - sweep)
                me = [get(h, b) for b in range(3)]
                back = [roll(x, 1) for x in me]
                ahead = [roll(x, -1) for x in me]
                for b in range(2 if edge or sweep == 2 else 3):
                    beside = jnp.where(sub == 0, back[b - 1], back[b]) + jnp.where(sub == 7, ahead[(b + 1) % 3], ahead[b])
                    beside = beside + (get(h - 1, b) + get(h + 1, b)) + lanes(me[b])
                    new = (1.0 - OMEGA) * me[b] + ring[0, parity, h + 2, b] + pr[h + 2, b] * beside
                    if sweep < 2:
                        ring[sweep + 1, parity, h + 2, b] = new
                    else:
                        new = new * iw[h, pl.ds(8 * b, 8), :]
                        for da in range(2):
                            for dh in range(2):
                                pe[parity, pl.ds(b * 128 + da * 8 + 2 * h + dh, 8, stride=16), :] = new

    def prolong(k, g, c, parity):
        acc = zero
        for a in range(angs):
            rows = pl.ds(8 * a, 8)
            r = res[k, c, rows, :]
            z = kf[rows, :] * r + pe[parity, rows, :]
            ys[k, c, rows, :] = z
            acc = acc + r * z
            vf[c, rows, :] = weight[rows, :] * z
        add_moment(g, c, 2 * k, acc)
        for i in range(4):
            fsu[c, pl.ds(8 * i, 8), :] = vf[c, pl.ds(64 * i + 7, 8, stride=8), :]
            fsd[c, pl.ds(8 * i, 8), :] = vf[c, pl.ds(64 * i, 8, stride=8), :]

    def precondition(k, g):
        deep_wait(k, g, g * per, per)

        def pair_body(i, carry):
            pair = g * (per // 2) + i
            for parity in range(2):
                sweeps(k, 2 * pair + parity, pair, parity)
            for parity in range(2):
                prolong(k, g, 2 * pair + parity, parity)
            return carry

        lax.fori_loop(0, per // 2, pair_body, 0)
        fine_start(k, g)

    def apply_fine(k, g):
        fine_wait(k, g)

        def column(i, carry):
            c = g * per + i
            acc = zero
            before, now = fl[k, c], vf[c, pl.ds(0, 8), :]
            for a in range(angs):
                rows = pl.ds(8 * a, 8)
                after = vf[c, pl.ds(8 * (a + 1), 8), :] if a < angs - 1 else fr[k, c]
                below = jnp.where(sub == 0, fd[k, c, pl.ds(a, 1), :], roll(now, 1))
                above = jnp.where(sub == 7, fu[k, c, pl.ds(a, 1), :], roll(now, -1))
                beside = (before + after) + (below + above) + lanes(now)
                z = ys[k, c, rows, :]
                r = diag[rows, :] * z - weight[rows, :] * beside - res[k, c, rows, :]
                res[k + 1, c, rows, :] = r
                acc = acc + r * z
                before, now = now, after
            add_moment(g, c, 2 * k + 1, acc)
            if k + 1 < STEPS:
                restrict(k + 1, c)
            return carry

        lax.fori_loop(0, per, column, 0)
        if k + 1 < STEPS:
            send_deep(k + 1, g)

    def psum_start(g, stage):
        n, me, slots = (na, me_a, pa) if stage == 0 else (nh, me_h, pb)

        def one(d, carry):
            other = lax.rem(me + d, n)
            where = {"ang": other, "hgt": me_h} if stage == 0 else {"ang": me_a, "hgt": other}
            pltpu.make_async_remote_copy(
                src_ref=tsum.at[g + stage * groups], dst_ref=slots.at[g, me],
                send_sem=psend.at[stage, g], recv_sem=precv.at[stage, g],
                device_id=where, device_id_type=MESH).start()
            return carry

        lax.fori_loop(1, n, one, 0)

    def psum_wait(g, stage):
        n, me, slots = (na, me_a, pa) if stage == 0 else (nh, me_h, pb)
        many = slots.at[g, pl.ds(0, n - 1)]
        pltpu.make_async_copy(many, many, psend.at[stage, g]).wait()
        pltpu.make_async_copy(many, many, precv.at[stage, g]).wait()
        slots[g, me] = tsum[g + stage * groups]
        total = slots[g, 0]
        for i in range(1, n):
            total = total + slots[g, i]
        return total

    for k in range(STEPS):
        lax.fori_loop(0, groups, lambda g, carry: (precondition(k, g), carry)[1], 0)
        if k + 1 < STEPS:
            lax.fori_loop(0, groups, lambda g, carry: (apply_fine(k, g), carry)[1], 0)

    def last(g, carry):
        apply_fine(STEPS - 1, g)
        psum_start(g, 0)
        return carry

    lax.fori_loop(0, groups, last, 0)

    def middle(g, carry):
        tsum[g + groups] = psum_wait(g, 0)
        psum_start(g, 1)
        return carry

    lax.fori_loop(0, groups, middle, 0)

    def out_copies(g):
        c = pl.ds(g * per, per)
        return (pltpu.make_async_copy(ys.at[0, c], out_x.at[c], out_sem.at[0, g]),
                pltpu.make_async_copy(res.at[0, c], out_r.at[c], out_sem.at[1, g]))

    def finish(g, carry):
        total = psum_wait(g, 1)
        m = [total[i:i + 1, :] for i in range(2 * STEPS)]
        none = jnp.zeros_like(m[0])
        one = jnp.ones_like(m[0])
        way, left, made = [one, none, none], [one, none, none, none], [none] * 3
        rz = m[0]
        for k in range(STEPS):
            image = [none] * 4
            for j in range(k + 1):
                image[j + 1] = image[j + 1] + way[j]
                image[j] = image[j] + way[j]
            curve = none
            for i in range(k + 1):
                for j in range(k + 2):
                    curve = curve + way[i] * image[j] * m[i + j]
            alpha = rz / curve
            made = [made[j] + alpha * way[j] for j in range(3)]
            left = [left[j] - alpha * image[j] for j in range(4)]
            if k + 1 < STEPS:
                new = none
                for i in range(k + 2):
                    for j in range(k + 2):
                        new = new + left[i] * left[j] * m[i + j]
                beta = new / rz
                way = [left[j] + beta * way[j] for j in range(3)]
                rz = new

        def column(i, carry):
            c = g * per + i

            def pick(x):
                return jnp.sum(jnp.where(lane[0:1] == c, x, 0.0), axis=1, keepdims=True)

            x_of = [jnp.broadcast_to(pick(x), T) for x in made]
            r_of = [jnp.broadcast_to(pick(x), T) for x in left]
            for a in range(angs):
                rows = pl.ds(8 * a, 8)
                x = x_of[0] * ys[0, c, rows, :] + x_of[1] * ys[1, c, rows, :] + x_of[2] * ys[2, c, rows, :]
                r = (r_of[0] * res[0, c, rows, :] + r_of[1] * res[1, c, rows, :]
                     + r_of[2] * res[2, c, rows, :] + r_of[3] * res[3, c, rows, :])
                ys[0, c, rows, :] = x
                res[0, c, rows, :] = r
            return carry

        lax.fori_loop(0, per, column, 0)
        for copy in out_copies(g):
            copy.start()
        return carry

    lax.fori_loop(0, groups, finish, 0)
    for g in range(groups):
        for copy in out_copies(g):
            copy.wait()


def body(loads, material, support, modulus, positions):
    cases, comps, angs, rows, radial = loads.shape
    cols = cases * comps
    na, nh = lax.axis_size("ang"), lax.axis_size("hgt")
    flat = angs * rows
    any_spec = pl.BlockSpec(memory_space=pl.ANY)
    smem = pl.BlockSpec(memory_space=pltpu.SMEM)
    out = jax.ShapeDtypeStruct((cols, flat, radial), F32)
    v = lambda *shape: pltpu.VMEM((*shape, 128), F32)
    dma = lambda *shape: pltpu.SemaphoreType.DMA(shape)
    x, r = pl.pallas_call(
        kernel,
        out_shape=(out, out),
        in_specs=[smem, smem, any_spec, any_spec, any_spec],
        out_specs=(any_spec, any_spec),
        scratch_shapes=[
            pltpu.VMEM((flat, 128), jnp.int32), pltpu.VMEM((flat, 128), jnp.int32),
            v(flat), v(flat), v(flat), v(flat), v(4, 16), v(4, 16),
            v(STEPS + 1, cols, flat), v(STEPS, cols, flat), v(cols, flat), v(2, flat),
            v(STEPS, cols + 1, 10, 16),
            v(cols + 1, 16), v(cols + 1, 16), v(4, cols // 2 + 1, 8),
            v(STEPS, cols + 1, 16), v(STEPS, cols + 1, 16), v(STEPS, 4, cols // 2 + 1, 8),
            v(8, 3, 8), v(3, 2, 8, 3, 8),
            v(cols, 32), v(cols, 32), v(STEPS, cols, 32), v(STEPS, cols, 32),
            v(STEPS, cols, 8), v(STEPS, cols, 8),
            v(2 * GROUPS, 8), v(GROUPS, na, 8), v(GROUPS, nh, 8),
            dma(GROUPS + 2), dma(STEPS, GROUPS + 1, 8), dma(STEPS, GROUPS + 1, 8),
            dma(STEPS, GROUPS, 4), dma(STEPS, GROUPS, 4), dma(2, GROUPS), dma(2, GROUPS), dma(2, GROUPS),
        ],
        compiler_params=pltpu.CompilerParams(
            collective_id=0, has_side_effects=True, vmem_limit_bytes=60 * 1024 * 1024),
        name="girder_cg",
    )(modulus, positions, loads.reshape(cols, flat, radial), material.reshape(flat, radial), support.reshape(flat, radial))
    return x.reshape(loads.shape), r.reshape(loads.shape)


def solution(mesh):
    field = P(None, None, "ang", "hgt", None)
    cell = P("ang", "hgt", None)
    return jax.shard_map(body, mesh=mesh, in_specs=(field, cell, cell, P(), P()),
                         out_specs=(field, field), check_vma=False)
```

```python
import functools

import jax
import jax.numpy as jnp
from jax import lax
from jax.experimental import pallas as pl
from jax.experimental.pallas import tpu as pltpu
from jax.sharding import PartitionSpec as P

STEPS = 3
SIGMA = 6.5
SPRING = 20.0
OMEGA = 0.8
LOAD = 3.0
GROUPS = 6
MESH = pl.DeviceIdType.MESH
F32 = jnp.float32
T = (8, 128)
UP, DOWN, RIGHT, LEFT, RU, LU, RD, LD = range(8)
SHIFT = ((0, 1), (0, -1), (1, 0), (-1, 0), (1, 1), (-1, 1), (1, -1), (-1, -1))


def kernel(
    modulus, positions, loads, material, support,
    res, ys, sums,
    mat, sup, weight, spring, diag, kf, kv, iw,
    vf, pe, co, sr, sl, sc, hl, hr, rc, pr, ring,
    fsu, fsd, fu, fd, fl, fr, moments, tsum, pa, pb,
    in_sem, dsend, drecv, fsend, frecv, psend, precv,
):
    na, nh = lax.axis_size("ang"), lax.axis_size("hgt")
    me_a, me_h = lax.axis_index("ang"), lax.axis_index("hgt")
    cols = loads.shape[0]
    groups = GROUPS
    per = cols // groups
    pcol = cols
    angs = 32
    sub = lax.broadcasted_iota(jnp.int32, T, 0)
    lane = lax.broadcasted_iota(jnp.int32, T, 1)
    has_up, has_down = me_h < nh - 1, me_h > 0

    def device(da, dh):
        return {"ang": lax.rem(me_a + da + na, na), "hgt": me_h + dh}

    def guarded(dh, body):
        if dh > 0:
            pl.when(has_up)(body)
        elif dh < 0:
            pl.when(has_down)(body)
        else:
            body()

    in_copies = [pltpu.make_async_copy(material, mat, in_sem.at[groups]),
                 pltpu.make_async_copy(support, sup, in_sem.at[groups + 1])]
    for copy in in_copies:
        copy.start()

    def load_copy(g):
        c = pl.ds(g * per, per)
        return pltpu.make_async_copy(loads.at[c], res.at[0, c], in_sem.at[g])

    for g in range(groups):
        load_copy(g).start()

    barrier = pltpu.get_barrier_semaphore()

    def greet_a(d, carry):
        pl.semaphore_signal(barrier, inc=1, device_id={"ang": lax.rem(me_a + d, na), "hgt": me_h}, device_id_type=MESH)
        return carry

    def greet_h(d, carry):
        pl.semaphore_signal(barrier, inc=1, device_id={"ang": me_a, "hgt": lax.rem(me_h + d, nh)}, device_id_type=MESH)
        return carry

    for da, dh in SHIFT[4:]:
        guarded(dh, lambda da=da, dh=dh: pl.semaphore_signal(
            barrier, inc=1, device_id=device(da, dh), device_id_type=MESH))
    lax.fori_loop(1, na, greet_a, 0)
    lax.fori_loop(1, nh, greet_h, 0)

    def roll(x, shift, axis=0):
        return pltpu.roll(x, shift % x.shape[axis], axis)

    def lanes(v):
        return jnp.where(lane == 0, 0.0, roll(v, 1, 1)) + jnp.where(lane == 127, 0.0, roll(v, -1, 1))

    def quad(ref, j, b, *lead):
        total = None
        for da in range(2):
            for dh in range(2):
                part = ref[(*lead, pl.ds(b * 128 + da * 8 + 2 * j + dh, 8, stride=16), slice(None))]
                total = part if total is None else total + part
        return total

    zero = jnp.zeros(T, F32)

    def clear(row, corners, fine):
        def one(c, carry):
            for k in range(STEPS):
                for j in range(3):
                    for b in range(2):
                        co[k, c, row + j, pl.ds(8 * b, 8), :] = zero
            return carry

        lax.fori_loop(0, cols + 1, one, 0)

        def two(c, carry):
            for k in range(STEPS):
                for i in range(4):
                    fine[k, c, pl.ds(8 * i, 8), :] = zero
            return carry

        lax.fori_loop(0, cols, two, 0)

        def three(c, carry):
            for k in range(STEPS):
                for d in corners:
                    rc[k, d, c] = zero
            return carry

        lax.fori_loop(0, cols // 2 + 1, three, 0)

    def deep(k, slot, first, count, d):
        c = pl.ds(first, count)
        pair = pl.ds(first // 2, (count + 1) // 2)
        if d == UP:
            src, dst = co.at[k, c, pl.ds(4, 3)], co.at[k, c, pl.ds(0, 3)]
        elif d == DOWN:
            src, dst = co.at[k, c, pl.ds(3, 3)], co.at[k, c, pl.ds(7, 3)]
        elif d == RIGHT:
            src, dst = sr.at[c], hl.at[k, c]
        elif d == LEFT:
            src, dst = sl.at[c], hr.at[k, c]
        else:
            src, dst = sc.at[d - 4, pair], rc.at[k, d - 4, pair]
        return pltpu.make_async_remote_copy(
            src_ref=src, dst_ref=dst, send_sem=dsend.at[k, slot, d], recv_sem=drecv.at[k, slot, d],
            device_id=device(*SHIFT[d]), device_id_type=MESH)

    def deep_start(k, slot, first, count):
        for d in (UP, DOWN, RU, LU, RD, LD, RIGHT, LEFT):
            guarded(SHIFT[d][1], lambda d=d: deep(k, slot, first, count, d).start())

    def deep_wait(k, slot, first, count):
        for d in range(8):
            guarded(SHIFT[d][1], lambda d=d: deep(k, slot, first, count, d).wait_send())
            guarded(-SHIFT[d][1], lambda d=d: deep(k, slot, first, count, d).wait_recv())

    def fine(k, g, d):
        c = pl.ds(g * per, per)
        if d == UP:
            src, dst = fsu.at[c], fd.at[k, c]
        elif d == DOWN:
            src, dst = fsd.at[c], fu.at[k, c]
        elif d == RIGHT:
            src, dst = vf.at[c, pl.ds(8 * (angs - 1), 8)], fl.at[k, c]
        else:
            src, dst = vf.at[c, pl.ds(0, 8)], fr.at[k, c]
        return pltpu.make_async_remote_copy(
            src_ref=src, dst_ref=dst, send_sem=fsend.at[k, g, d], recv_sem=frecv.at[k, g, d],
            device_id=device(*SHIFT[d]), device_id_type=MESH)

    def fine_start(k, g):
        for d in range(4):
            guarded(SHIFT[d][1], lambda d=d: fine(k, g, d).start())

    def fine_wait(k, g):
        for d in range(4):
            guarded(SHIFT[d][1], lambda d=d: fine(k, g, d).wait_send())
            guarded(-SHIFT[d][1], lambda d=d: fine(k, g, d).wait_recv())

    def corner_tiles(k, c):
        low = [co[k, c, 3 + h, pl.ds(0, 8), :] for h in range(4)]
        high = [co[k, c, 3 + h, pl.ds(8, 8), :] for h in range(4)]
        for t in range(2):
            sr[c, pl.ds(8 * t, 8), :] = jnp.where(sub < 4, roll(high[2 * t], 4), high[2 * t + 1])
            sl[c, pl.ds(8 * t, 8), :] = jnp.where(sub < 4, low[2 * t], roll(low[2 * t + 1], 4))
        return (
            jnp.where(sub == 5, roll(high[2], -2), high[3]),
            jnp.where(sub == 2, roll(low[2], 2), low[3]),
            jnp.where(sub == 5, roll(high[1], -2), high[0]),
            jnp.where(sub == 2, roll(low[1], 2), low[0]),
        )

    def merge(d, even, odd):
        if d in (RU, RD):
            return jnp.where(sub < 4, roll(even, 4), odd)
        return jnp.where(sub < 4, even, roll(odd, 4))

    def pack_pair(k, pair):
        even, odd = corner_tiles(k, 2 * pair), corner_tiles(k, 2 * pair + 1)
        for d in (RU, LU, RD, LD):
            sc[d - 4, pair] = merge(d, even[d - 4], odd[d - 4])

    def halo(k, c, pair, parity, h):
        if 0 <= h < 4:
            t = h // 2
            q, p = hr[k, c, pl.ds(8 * t, 8), :], hl[k, c, pl.ds(8 * t, 8), :]
            if h % 2 == 0:
                return jnp.where(sub < 4, q, roll(p, 4))
            return jnp.where(sub < 4, roll(q, 4), p)
        left = rc[k, (RU if h < 0 else RD) - 4, pair]
        right = rc[k, (LU if h < 0 else LD) - 4, pair]
        if parity == 0:
            left = roll(left, 4)
        else:
            right = roll(right, 4)
        if h in (-2, 5):
            left, right = roll(left, 2), roll(right, -2)
        return jnp.where(sub < 4, right, left)

    def ring_row(k, c, pair, parity, h):
        return [co[k, c, 3 + h, pl.ds(0, 8), :], co[k, c, 3 + h, pl.ds(8, 8), :], halo(k, c, pair, parity, h)]

    for copy in in_copies:
        copy.wait()

    def weigh(a, carry):
        rows = pl.ds(pl.multiple_of(a * 8, 8), 8)
        kind = mat[rows, :]
        stiff = zero
        for level in range(modulus.shape[0]):
            stiff = stiff + jnp.where(kind == level, modulus[level], 0.0)
        w = jnp.sqrt(stiff)
        s = sup[rows, :].astype(F32)
        d = SIGMA * w * w + SPRING * s
        weight[rows, :] = w
        spring[rows, :] = s
        diag[rows, :] = d
        kf[rows, :] = OMEGA / d
        return carry

    lax.fori_loop(0, angs, weigh, 0, unroll=4)
    for j in range(4):
        for b in range(2):
            wc = 0.25 * quad(weight, j, b)
            s = 0.25 * quad(spring, j, b)
            kd = OMEGA / (SIGMA * wc * wc + SPRING * s)
            kv[j, pl.ds(8 * b, 8), :] = 0.5 * wc * kd
            iw[j, pl.ds(8 * b, 8), :] = 0.5 / wc
            co[0, pcol, 3 + j, pl.ds(8 * b, 8), :] = wc * wc * kd
    tiles = corner_tiles(0, pcol)
    for d in (RU, LU, RD, LD):
        sc[d - 4, pcol // 2] = merge(d, tiles[d - 4], zero)

    diagonals = 2 * (has_up.astype(jnp.int32) + has_down.astype(jnp.int32))
    pl.semaphore_wait(barrier, na - 1 + nh - 1 + diagonals)
    deep_start(0, groups, pcol, 1)

    def restrict(k, c):
        for j in range(4):
            for b in range(2):
                co[k, c, 3 + j, pl.ds(8 * b, 8), :] = kv[j, pl.ds(8 * b, 8), :] * quad(res, j, b, k, c)

    def send_deep(k, g):
        lax.fori_loop(0, per // 2, lambda i, carry: (pack_pair(k, g * (per // 2) + i), carry)[1], 0)
        deep_start(k, g, g * per, per)

    total_angles = na * angs

    def first(g):
        load_copy(g).wait()

        def column(i, carry):
            c = g * per + i
            amount = jnp.where(lax.rem(c, 3) == 2, -LOAD, 0.0)
            spot = jnp.full(T, me_a * angs, jnp.int32) - positions[c // 3]
            for a in range(angs):
                apart = jnp.abs(spot + a)
                near = jnp.minimum(apart, total_angles - apart) < angs
                res[0, c, pl.ds(8 * a, 8), :] += jnp.where(near, amount, 0.0)
            restrict(0, c)
            return carry

        lax.fori_loop(0, per, column, 0)
        send_deep(0, g)

    def coarse_ring():
        deep_wait(0, groups, pcol, 1)
        for h in range(-2, 6):
            row = ring_row(0, pcol, pcol // 2, 0, h)
            for b in range(3):
                pr[h + 2, b] = row[b]

    def sweeps(k, c, pair, parity):
        v0 = {h: ring_row(k, c, pair, parity, h) for h in range(-2, 6)}
        for h in range(-2, 6):
            for b in range(3):
                ring[0, parity, h + 2, b] = v0[h][b]
        outer = {h: [co[k, c, 3 + h, pl.ds(0, 8), :], co[k, c, 3 + h, pl.ds(8, 8), :]] for h in (-3, 6)}
        for sweep in range(3):
            def get(h, b):
                if h in outer:
                    return outer[h][b]
                return ring[sweep, parity, h + 2, b]

            for h in range(-2 + sweep, 6 - sweep):
                edge = h in (-2 + sweep, 5 - sweep)
                me = [get(h, b) for b in range(3)]
                back = [roll(x, 1) for x in me]
                ahead = [roll(x, -1) for x in me]
                for b in range(2 if edge or sweep == 2 else 3):
                    beside = jnp.where(sub == 0, back[b - 1], back[b]) + jnp.where(sub == 7, ahead[(b + 1) % 3], ahead[b])
                    beside = beside + (get(h - 1, b) + get(h + 1, b)) + lanes(me[b])
                    new = (1.0 - OMEGA) * me[b] + ring[0, parity, h + 2, b] + pr[h + 2, b] * beside
                    if sweep < 2:
                        ring[sweep + 1, parity, h + 2, b] = new
                    else:
                        new = new * iw[h, pl.ds(8 * b, 8), :]
                        for da in range(2):
                            for dh in range(2):
                                pe[parity, pl.ds(b * 128 + da * 8 + 2 * h + dh, 8, stride=16), :] = new

    def prolong(k, g, c, parity):
        acc = zero
        for a in range(angs):
            rows = pl.ds(8 * a, 8)
            r = res[k, c, rows, :]
            z = kf[rows, :] * r + pe[parity, rows, :]
            ys[k, c, rows, :] = z
            acc = acc + r * z
            vf[c, rows, :] = weight[rows, :] * z
        moments[c, 2 * k] = acc
        for i in range(4):
            fsu[c, pl.ds(8 * i, 8), :] = vf[c, pl.ds(64 * i + 7, 8, stride=8), :]
            fsd[c, pl.ds(8 * i, 8), :] = vf[c, pl.ds(64 * i, 8, stride=8), :]

    def precondition(k, g):
        deep_wait(k, g, g * per, per)

        def pair_body(i, carry):
            pair = g * (per // 2) + i
            for parity in range(2):
                sweeps(k, 2 * pair + parity, pair, parity)
            for parity in range(2):
                prolong(k, g, 2 * pair + parity, parity)
            return carry

        lax.fori_loop(0, per // 2, pair_body, 0)
        fine_start(k, g)

    def apply_fine(k, g):
        fine_wait(k, g)

        def column(i, carry):
            c = g * per + i
            acc = zero
            before, now = fl[k, c], vf[c, pl.ds(0, 8), :]
            for a in range(angs):
                rows = pl.ds(8 * a, 8)
                after = vf[c, pl.ds(8 * (a + 1), 8), :] if a < angs - 1 else fr[k, c]
                below = jnp.where(sub == 0, fd[k, c, pl.ds(a, 1), :], roll(now, 1))
                above = jnp.where(sub == 7, fu[k, c, pl.ds(a, 1), :], roll(now, -1))
                beside = (before + after) + (below + above) + lanes(now)
                z = ys[k, c, rows, :]
                r = diag[rows, :] * z - weight[rows, :] * beside - res[k, c, rows, :]
                res[k + 1, c, rows, :] = r
                acc = acc + r * z
                before, now = now, after
            moments[c, 2 * k + 1] = acc
            if k + 1 < STEPS:
                restrict(k + 1, c)
            return carry

        lax.fori_loop(0, per, column, 0)
        if k + 1 < STEPS:
            send_deep(k + 1, g)

    def reduce_moments(g):
        for i in range(per):
            c = g * per + i
            rows = zero
            for m in range(2 * STEPS):
                rows = jnp.where(sub == m, jnp.sum(moments[c, m], axis=0, keepdims=True), rows)
            tsum[0] += jnp.where(lane == c, jnp.sum(rows, axis=1, keepdims=True), 0.0)

    def psum(stage):
        n, me, slots = (na, me_a, pa) if stage == 0 else (nh, me_h, pb)

        def one(d, carry):
            other = lax.rem(me + d, n)
            where = {"ang": other, "hgt": me_h} if stage == 0 else {"ang": me_a, "hgt": other}
            pltpu.make_async_remote_copy(
                src_ref=tsum.at[stage], dst_ref=slots.at[me], send_sem=psend.at[stage], recv_sem=precv.at[stage],
                device_id=where, device_id_type=MESH).start()
            return carry

        lax.fori_loop(1, n, one, 0)
        slots[me] = tsum[stage]
        many = slots.at[pl.ds(0, n - 1)]
        pltpu.make_async_copy(many, many, psend.at[stage]).wait()
        pltpu.make_async_copy(many, many, precv.at[stage]).wait()
        total = slots[0]
        for i in range(1, n):
            total = total + slots[i]
        return total

    def stage(s, g):
        if s == 0:
            first(g)
        elif s % 2:
            precondition(s // 2, g)
        else:
            apply_fine(s // 2 - 1, g)
            if s == 2 * STEPS:
                reduce_moments(g)

    tsum[0] = zero
    for t in range(2 * STEPS + 2):
        if t == 1:
            pl.when(jnp.logical_not(has_down))(lambda: clear(0, (RU - 4, LU - 4), fd))
            pl.when(jnp.logical_not(has_up))(lambda: clear(7, (RD - 4, LD - 4), fu))
            coarse_ring()

        def both(i, carry):
            if t <= 2 * STEPS:
                stage(t, 2 * i)
            if t >= 1:
                stage(t - 1, 2 * i + 1)
            return carry

        lax.fori_loop(0, groups // 2, both, 0)

    tsum[1] = psum(0)
    sums[...] = psum(1)


def combine(sums, res, ys, out_x, out_r):
    m = [sums[i:i + 1, :] for i in range(2 * STEPS)]
    none = jnp.zeros_like(m[0])
    one = jnp.ones_like(m[0])
    way, left, made = [one, none, none], [one, none, none, none], [none] * 3
    rz = m[0]
    for k in range(STEPS):
        image = [none] * 4
        for j in range(k + 1):
            image[j + 1] = image[j + 1] + way[j]
            image[j] = image[j] + way[j]
        curve = none
        for i in range(k + 1):
            for j in range(k + 2):
                curve = curve + way[i] * image[j] * m[i + j]
        alpha = rz / curve
        made = [made[j] + alpha * way[j] for j in range(3)]
        left = [left[j] - alpha * image[j] for j in range(4)]
        if k + 1 < STEPS:
            new = none
            for i in range(k + 2):
                for j in range(k + 2):
                    new = new + left[i] * left[j] * m[i + j]
            beta = new / rz
            way = [left[j] + beta * way[j] for j in range(3)]
            rz = new

    c = pl.program_id(0)
    lane = lax.broadcasted_iota(jnp.int32, (1, 128), 1)

    def pick(x):
        return jnp.broadcast_to(jnp.sum(jnp.where(lane == c, x, 0.0), axis=1, keepdims=True), T)

    x_of = [pick(x) for x in made]
    r_of = [pick(x) for x in left]
    for a in range(out_x.shape[1] // 8):
        rows = pl.ds(8 * a, 8)
        out_x[0, rows, :] = x_of[0] * ys[0, c, rows, :] + x_of[1] * ys[1, c, rows, :] + x_of[2] * ys[2, c, rows, :]
        out_r[0, rows, :] = (r_of[0] * res[0, c, rows, :] + r_of[1] * res[1, c, rows, :]
                             + r_of[2] * res[2, c, rows, :] + r_of[3] * res[3, c, rows, :])


def body(loads, material, support, modulus, positions):
    cases, comps, angs, rows, radial = loads.shape
    cols = cases * comps
    na, nh = lax.axis_size("ang"), lax.axis_size("hgt")
    flat = angs * rows
    any_spec = pl.BlockSpec(memory_space=pltpu.HBM)
    smem = pl.BlockSpec(memory_space=pltpu.SMEM)
    vmem = pl.BlockSpec(memory_space=pltpu.VMEM)
    v = lambda *shape: pltpu.VMEM((*shape, 128), F32)
    dma = lambda *shape: pltpu.SemaphoreType.DMA(shape)
    res, ys, sums = pl.pallas_call(
        kernel,
        out_shape=(v(STEPS + 1, cols, flat), v(STEPS, cols, flat), v(8)),
        in_specs=[smem, smem, any_spec, any_spec, any_spec],
        out_specs=(vmem, vmem, vmem),
        scratch_shapes=[
            pltpu.VMEM((flat, 128), jnp.int32), pltpu.VMEM((flat, 128), jnp.int32),
            v(flat), v(flat), v(flat), v(flat), v(4, 16), v(4, 16),
            v(cols, flat), v(2, flat),
            v(STEPS, cols + 1, 10, 16),
            v(cols + 1, 16), v(cols + 1, 16), v(4, cols // 2 + 1, 8),
            v(STEPS, cols + 1, 16), v(STEPS, cols + 1, 16), v(STEPS, 4, cols // 2 + 1, 8),
            v(8, 3, 8), v(3, 2, 8, 3, 8),
            v(cols, 32), v(cols, 32), v(STEPS, cols, 32), v(STEPS, cols, 32),
            v(STEPS, cols, 8), v(STEPS, cols, 8),
            v(cols, 2 * STEPS, 8), v(2, 8), v(na, 8), v(nh, 8),
            dma(GROUPS + 2), dma(STEPS, GROUPS + 1, 8), dma(STEPS, GROUPS + 1, 8),
            dma(STEPS, GROUPS, 4), dma(STEPS, GROUPS, 4), dma(2), dma(2),
        ],
        compiler_params=pltpu.CompilerParams(
            collective_id=0, has_side_effects=True, vmem_limit_bytes=55 * 1000 * 1000),
        name="girder_cg",
    )(modulus, positions, loads.reshape(cols, flat, radial), material.reshape(flat, radial), support.reshape(flat, radial))
    out = jax.ShapeDtypeStruct((cols, flat, radial), F32)
    block = pl.BlockSpec((1, flat, radial), lambda c: (c, 0, 0))
    x, r = pl.pallas_call(
        combine,
        grid=(cols,),
        out_shape=(out, out),
        in_specs=[vmem, vmem, vmem],
        out_specs=(block, block),
        compiler_params=pltpu.CompilerParams(vmem_limit_bytes=16 * 1024 * 1024),
        name="girder_combine",
    )(sums, res, ys)
    return x.reshape(loads.shape), r.reshape(loads.shape)


def solution(mesh):
    field = P(None, None, "ang", "hgt", None)
    cell = P("ang", "hgt", None)
    return jax.shard_map(body, mesh=mesh, in_specs=(field, cell, cell, P(), P()),
                         out_specs=(field, field), check_vma=False)
```

```python
import functools

import jax
import jax.numpy as jnp
from jax import lax
from jax.experimental import pallas as pl
from jax.experimental.pallas import tpu as pltpu
from jax.sharding import PartitionSpec as P

STEPS = 3
SIGMA = 6.5
SPRING = 20.0
OMEGA = 0.8
LOAD = 3.0
GROUPS = 3
MESH = pl.DeviceIdType.MESH
F32 = jnp.float32
T = (8, 128)
UP, DOWN, RIGHT, LEFT, RU, LU, RD, LD = range(8)
SHIFT = ((0, 1), (0, -1), (1, 0), (-1, 0), (1, 1), (-1, 1), (1, -1), (-1, -1))


def kernel(
    modulus, positions, loads, material, support,
    res, ys, sums,
    mat, sup, weight, spring, diag, kf, kv, iw,
    vf, pe, co, sr, sl, sc, hl, hr, rc, pr, ring,
    fsu, fsd, fu, fd, fl, fr, moments, tsum, row, slots,
    spread, in_sem, dsend, drecv, fsend, frecv, psend, precv,
):
    na, nh = lax.axis_size("ang"), lax.axis_size("hgt")
    me_a, me_h = lax.axis_index("ang"), lax.axis_index("hgt")
    cols = loads.shape[0]
    groups = GROUPS
    per = cols // groups
    pcol = cols
    angs = 32
    sub = lax.broadcasted_iota(jnp.int32, T, 0)
    lane = lax.broadcasted_iota(jnp.int32, T, 1)
    has_up, has_down = me_h < nh - 1, me_h > 0

    def device(da, dh):
        return {"ang": lax.rem(me_a + da + na, na), "hgt": me_h + dh}

    def guarded(dh, body):
        if dh > 0:
            pl.when(has_up)(body)
        elif dh < 0:
            pl.when(has_down)(body)
        else:
            body()

    in_copies = [pltpu.make_async_copy(material, mat, in_sem.at[groups]),
                 pltpu.make_async_copy(support, sup, in_sem.at[groups + 1])]
    for copy in in_copies:
        copy.start()

    def load_copy(g):
        c = pl.ds(g * per, per)
        return pltpu.make_async_copy(loads.at[c], res.at[0, c], in_sem.at[g])

    for g in range(groups):
        load_copy(g).start()

    barrier = pltpu.get_barrier_semaphore()

    def neighbour(da, dh, sem):
        pl.semaphore_signal(sem, inc=1, device_id=device(da, dh), device_id_type=MESH)

    for da, dh in SHIFT:
        guarded(dh, lambda da=da, dh=dh: neighbour(da, dh, barrier))

    rounds = ([(0, 1 << i) for i in range((na // 2 - 1).bit_length())]
              + [(1, 1 << i) for i in range((nh - 1).bit_length())])

    def far(r, body):
        axis, d = rounds[r]
        if axis == 0:
            body(d, 0)
            body(-d, 0)
        else:
            pl.when(me_h + d < nh)(lambda: body(0, d))
            pl.when(me_h - d >= 0)(lambda: body(0, -d))

    def tell(r):
        if r < len(rounds):
            far(r, lambda da, dh: neighbour(da, dh, spread.at[r]))

    def hear(r):
        if r < len(rounds):
            axis, d = rounds[r]
            many = 2 if axis == 0 else (me_h + d < nh).astype(jnp.int32) + (me_h - d >= 0).astype(jnp.int32)
            pl.semaphore_wait(spread.at[r], many)

    def roll(x, shift, axis=0):
        return pltpu.roll(x, shift % x.shape[axis], axis)

    def lanes(v):
        return jnp.where(lane == 0, 0.0, roll(v, 1, 1)) + jnp.where(lane == 127, 0.0, roll(v, -1, 1))

    def quad(ref, j, b, *lead):
        total = None
        for da in range(2):
            for dh in range(2):
                part = ref[(*lead, pl.ds(b * 128 + da * 8 + 2 * j + dh, 8, stride=16), slice(None))]
                total = part if total is None else total + part
        return total

    zero = jnp.zeros(T, F32)

    def clear(row, corners, fine):
        def one(c, carry):
            for k in range(STEPS):
                for j in range(3):
                    for b in range(2):
                        co[k, c, row + j, pl.ds(8 * b, 8), :] = zero
            return carry

        lax.fori_loop(0, cols + 1, one, 0)

        def two(c, carry):
            for k in range(STEPS):
                for i in range(4):
                    fine[k, c, pl.ds(8 * i, 8), :] = zero
            return carry

        lax.fori_loop(0, cols, two, 0)

        def three(c, carry):
            for k in range(STEPS):
                for d in corners:
                    rc[k, d, c] = zero
            return carry

        lax.fori_loop(0, cols // 2 + 1, three, 0)

    def deep(k, slot, first, count, d):
        c = pl.ds(first, count)
        pair = pl.ds(first // 2, (count + 1) // 2)
        if d == UP:
            src, dst = co.at[k, c, pl.ds(4, 3)], co.at[k, c, pl.ds(0, 3)]
        elif d == DOWN:
            src, dst = co.at[k, c, pl.ds(3, 3)], co.at[k, c, pl.ds(7, 3)]
        elif d == RIGHT:
            src, dst = sr.at[c], hl.at[k, c]
        elif d == LEFT:
            src, dst = sl.at[c], hr.at[k, c]
        else:
            src, dst = sc.at[d - 4, pair], rc.at[k, d - 4, pair]
        return pltpu.make_async_remote_copy(
            src_ref=src, dst_ref=dst, send_sem=dsend.at[k, slot, d], recv_sem=drecv.at[k, slot, d],
            device_id=device(*SHIFT[d]), device_id_type=MESH)

    def deep_start(k, slot, first, count):
        for d in (RU, LU, RD, LD, RIGHT, LEFT, UP, DOWN):
            guarded(SHIFT[d][1], lambda d=d: deep(k, slot, first, count, d).start())

    def deep_wait(k, slot, first, count):
        for d in range(8):
            guarded(SHIFT[d][1], lambda d=d: deep(k, slot, first, count, d).wait_send())
            guarded(-SHIFT[d][1], lambda d=d: deep(k, slot, first, count, d).wait_recv())

    def fine(k, g, d):
        c = pl.ds(g * per, per)
        if d == UP:
            src, dst = fsu.at[c], fd.at[k, c]
        elif d == DOWN:
            src, dst = fsd.at[c], fu.at[k, c]
        elif d == RIGHT:
            src, dst = vf.at[c, pl.ds(8 * (angs - 1), 8)], fl.at[k, c]
        else:
            src, dst = vf.at[c, pl.ds(0, 8)], fr.at[k, c]
        return pltpu.make_async_remote_copy(
            src_ref=src, dst_ref=dst, send_sem=fsend.at[k, g, d], recv_sem=frecv.at[k, g, d],
            device_id=device(*SHIFT[d]), device_id_type=MESH)

    def fine_start(k, g):
        for d in (RIGHT, LEFT, UP, DOWN):
            guarded(SHIFT[d][1], lambda d=d: fine(k, g, d).start())

    def fine_wait(k, g):
        for d in range(4):
            guarded(SHIFT[d][1], lambda d=d: fine(k, g, d).wait_send())
            guarded(-SHIFT[d][1], lambda d=d: fine(k, g, d).wait_recv())

    def corner_tiles(k, c):
        low = [co[k, c, 3 + h, pl.ds(0, 8), :] for h in range(4)]
        high = [co[k, c, 3 + h, pl.ds(8, 8), :] for h in range(4)]
        for t in range(2):
            sr[c, pl.ds(8 * t, 8), :] = jnp.where(sub < 4, roll(high[2 * t], 4), high[2 * t + 1])
            sl[c, pl.ds(8 * t, 8), :] = jnp.where(sub < 4, low[2 * t], roll(low[2 * t + 1], 4))
        return (
            jnp.where(sub == 5, roll(high[2], -2), high[3]),
            jnp.where(sub == 2, roll(low[2], 2), low[3]),
            jnp.where(sub == 5, roll(high[1], -2), high[0]),
            jnp.where(sub == 2, roll(low[1], 2), low[0]),
        )

    def merge(d, even, odd):
        if d in (RU, RD):
            return jnp.where(sub < 4, roll(even, 4), odd)
        return jnp.where(sub < 4, even, roll(odd, 4))

    def pack_pair(k, pair):
        even, odd = corner_tiles(k, 2 * pair), corner_tiles(k, 2 * pair + 1)
        for d in (RU, LU, RD, LD):
            sc[d - 4, pair] = merge(d, even[d - 4], odd[d - 4])

    def halo(k, c, pair, parity, h):
        if 0 <= h < 4:
            t = h // 2
            q, p = hr[k, c, pl.ds(8 * t, 8), :], hl[k, c, pl.ds(8 * t, 8), :]
            if h % 2 == 0:
                return jnp.where(sub < 4, q, roll(p, 4))
            return jnp.where(sub < 4, roll(q, 4), p)
        left = rc[k, (RU if h < 0 else RD) - 4, pair]
        right = rc[k, (LU if h < 0 else LD) - 4, pair]
        if parity == 0:
            left = roll(left, 4)
        else:
            right = roll(right, 4)
        if h in (-2, 5):
            left, right = roll(left, 2), roll(right, -2)
        return jnp.where(sub < 4, right, left)

    def ring_row(k, c, pair, parity, h):
        return [co[k, c, 3 + h, pl.ds(0, 8), :], co[k, c, 3 + h, pl.ds(8, 8), :], halo(k, c, pair, parity, h)]

    for copy in in_copies:
        copy.wait()

    def weigh(a, carry):
        rows = pl.ds(pl.multiple_of(a * 8, 8), 8)
        kind = mat[rows, :]
        stiff = zero
        for level in range(modulus.shape[0]):
            stiff = stiff + jnp.where(kind == level, modulus[level], 0.0)
        w = jnp.sqrt(stiff)
        s = sup[rows, :].astype(F32)
        d = SIGMA * w * w + SPRING * s
        weight[rows, :] = w
        spring[rows, :] = s
        diag[rows, :] = d
        kf[rows, :] = OMEGA / d
        return carry

    lax.fori_loop(0, angs, weigh, 0, unroll=4)
    for j in range(4):
        for b in range(2):
            wc = 0.25 * quad(weight, j, b)
            s = 0.25 * quad(spring, j, b)
            kd = OMEGA / (SIGMA * wc * wc + SPRING * s)
            kv[j, pl.ds(8 * b, 8), :] = 0.5 * wc * kd
            iw[j, pl.ds(8 * b, 8), :] = 0.5 / wc
            co[0, pcol, 3 + j, pl.ds(8 * b, 8), :] = wc * wc * kd
    tiles = corner_tiles(0, pcol)
    for d in (RU, LU, RD, LD):
        sc[d - 4, pcol // 2] = merge(d, tiles[d - 4], zero)

    sides = has_up.astype(jnp.int32) + has_down.astype(jnp.int32)
    pl.semaphore_wait(barrier, 2 + 3 * sides)
    tell(0)
    deep_start(0, groups, pcol, 1)

    def restrict(k, c):
        for j in range(4):
            for b in range(2):
                co[k, c, 3 + j, pl.ds(8 * b, 8), :] = kv[j, pl.ds(8 * b, 8), :] * quad(res, j, b, k, c)

    def send_deep(k, g):
        lax.fori_loop(0, per // 2, lambda i, carry: (pack_pair(k, g * (per // 2) + i), carry)[1], 0)
        deep_start(k, g, g * per, per)

    total_angles = na * angs

    def first(g):
        load_copy(g).wait()

        def column(i, carry):
            c = g * per + i
            amount = jnp.where(lax.rem(c, 3) == 2, -LOAD, 0.0)
            spot = jnp.full(T, me_a * angs, jnp.int32) - positions[c // 3]
            for a in range(angs):
                apart = jnp.abs(spot + a)
                near = jnp.minimum(apart, total_angles - apart) < angs
                res[0, c, pl.ds(8 * a, 8), :] += jnp.where(near, amount, 0.0)
            restrict(0, c)
            return carry

        lax.fori_loop(0, per, column, 0)
        send_deep(0, g)

    def coarse_ring():
        deep_wait(0, groups, pcol, 1)
        for h in range(-2, 6):
            row = ring_row(0, pcol, pcol // 2, 0, h)
            for b in range(3):
                pr[h + 2, b] = row[b]

    def sweeps(k, c, pair, parity):
        v0 = {h: ring_row(k, c, pair, parity, h) for h in range(-2, 6)}
        for h in range(-2, 6):
            for b in range(3):
                ring[0, parity, h + 2, b] = v0[h][b]
        outer = {h: [co[k, c, 3 + h, pl.ds(0, 8), :], co[k, c, 3 + h, pl.ds(8, 8), :]] for h in (-3, 6)}
        for sweep in range(3):
            def get(h, b):
                if h in outer:
                    return outer[h][b]
                return ring[sweep, parity, h + 2, b]

            for h in range(-2 + sweep, 6 - sweep):
                edge = h in (-2 + sweep, 5 - sweep)
                me = [get(h, b) for b in range(3)]
                back = [roll(x, 1) for x in me]
                ahead = [roll(x, -1) for x in me]
                for b in range(2 if edge or sweep == 2 else 3):
                    beside = jnp.where(sub == 0, back[b - 1], back[b]) + jnp.where(sub == 7, ahead[(b + 1) % 3], ahead[b])
                    beside = beside + (get(h - 1, b) + get(h + 1, b)) + lanes(me[b])
                    new = (1.0 - OMEGA) * me[b] + ring[0, parity, h + 2, b] + pr[h + 2, b] * beside
                    if sweep < 2:
                        ring[sweep + 1, parity, h + 2, b] = new
                    else:
                        new = new * iw[h, pl.ds(8 * b, 8), :]
                        for da in range(2):
                            for dh in range(2):
                                pe[parity, pl.ds(b * 128 + da * 8 + 2 * h + dh, 8, stride=16), :] = new

    def prolong(k, g, c, parity):
        acc = zero
        for a in range(angs):
            rows = pl.ds(8 * a, 8)
            r = res[k, c, rows, :]
            z = kf[rows, :] * r + pe[parity, rows, :]
            ys[k, c, rows, :] = z
            acc = acc + r * z
            vf[c, rows, :] = weight[rows, :] * z
        moments[c, 2 * k] = acc
        for i in range(4):
            fsu[c, pl.ds(8 * i, 8), :] = vf[c, pl.ds(64 * i + 7, 8, stride=8), :]
            fsd[c, pl.ds(8 * i, 8), :] = vf[c, pl.ds(64 * i, 8, stride=8), :]

    def precondition(k, g):
        deep_wait(k, g, g * per, per)

        def pair_body(i, carry):
            pair = g * (per // 2) + i
            for parity in range(2):
                sweeps(k, 2 * pair + parity, pair, parity)
            for parity in range(2):
                prolong(k, g, 2 * pair + parity, parity)
            return carry

        lax.fori_loop(0, per // 2, pair_body, 0)
        fine_start(k, g)

    def apply_fine(k, g):
        fine_wait(k, g)

        def column(i, carry):
            c = g * per + i
            acc = zero
            before, now = fl[k, c], vf[c, pl.ds(0, 8), :]
            for a in range(angs):
                rows = pl.ds(8 * a, 8)
                after = vf[c, pl.ds(8 * (a + 1), 8), :] if a < angs - 1 else fr[k, c]
                below = jnp.where(sub == 0, fd[k, c, pl.ds(a, 1), :], roll(now, 1))
                above = jnp.where(sub == 7, fu[k, c, pl.ds(a, 1), :], roll(now, -1))
                beside = (before + after) + (below + above) + lanes(now)
                z = ys[k, c, rows, :]
                r = diag[rows, :] * z - weight[rows, :] * beside - res[k, c, rows, :]
                res[k + 1, c, rows, :] = r
                acc = acc + r * z
                before, now = now, after
            moments[c, 2 * k + 1] = acc
            if k + 1 < STEPS:
                restrict(k + 1, c)
            return carry

        lax.fori_loop(0, per, column, 0)
        if k + 1 < STEPS:
            send_deep(k + 1, g)

    def reduce_moments(g):
        for i in range(per):
            c = g * per + i
            rows = zero
            for m in range(2 * STEPS):
                rows = jnp.where(sub == m, jnp.sum(moments[c, m], axis=0, keepdims=True), rows)
            tsum[...] += jnp.where(lane == sub * cols + c, jnp.sum(rows, axis=1, keepdims=True), 0.0)

    def total_moments():
        n, me = na * nh, me_a * nh + me_h
        row[0] = jnp.sum(tsum[...], axis=0, keepdims=True)

        core, x, z_hi = lax.rem(me_a, 2), lax.rem(me_a // 2, na // 4), me_a // (na // 2)
        y, z = lax.rem(me_h, nh // 2), 2 * z_hi + me_h // (nh // 2)
        nx, ny = na // 4, nh // 2

        def order(q):
            return jnp.where(q == 0, 2, jnp.where(q == 1, 1, jnp.where(q == 2, 3, 0)))

        def one(i, carry):
            to_core = lax.rem(core + 1 - lax.rem(i, 2), 2)
            to_x = lax.rem(x + order(lax.rem(i // 2, nx)), nx)
            to_y = lax.rem(y + order(lax.rem(i // (2 * nx), ny)), ny)
            to_z = lax.rem(z + order(i // (2 * nx * ny)), 4)
            to = {"ang": (to_z // 2 * nx + to_x) * 2 + to_core, "hgt": lax.rem(to_z, 2) * ny + to_y}
            pltpu.make_async_remote_copy(
                src_ref=row.at[0], dst_ref=slots.at[me], send_sem=psend, recv_sem=precv,
                device_id=to, device_id_type=MESH).start()
            return carry

        lax.fori_loop(0, n - 1, one, 0)
        slots[me] = row[0]
        many = slots.at[pl.ds(0, n - 1)]
        pltpu.make_async_copy(many, many, psend).wait()
        pltpu.make_async_copy(many, many, precv).wait()
        parts = [slots[i] for i in range(8)]
        for i in range(8, n):
            parts[i % 8] = parts[i % 8] + slots[i]
        while len(parts) > 1:
            parts = [x + y for x, y in zip(parts[::2], parts[1::2])]
        return parts[0]

    def stage(s, g):
        if s == 0:
            first(g)
        elif s % 2:
            precondition(s // 2, g)
        else:
            apply_fine(s // 2 - 1, g)
            if s == 2 * STEPS:
                reduce_moments(g)

    tsum[...] = zero
    for t in range(2 * STEPS + 1):
        if t == 1:
            pl.when(jnp.logical_not(has_down))(lambda: clear(0, (RU - 4, LU - 4), fd))
            pl.when(jnp.logical_not(has_up))(lambda: clear(7, (RD - 4, LD - 4), fu))
            coarse_ring()
        lax.fori_loop(0, groups, lambda g, carry: (stage(t, g), carry)[1], 0)
        for r in range(2 * t - 2, 2 * t):
            if r >= 0:
                hear(r)
                tell(r + 1)

    sums[...] = total_moments()


def combine(sums, res, ys, out_x, out_r, coef, xs, rs, sem):
    cols, flat, _ = out_x.shape
    shape = (16, 128)
    sub = lax.broadcasted_iota(jnp.int32, shape, 0)
    lane = lax.broadcasted_iota(jnp.int32, shape, 1)
    m = [jnp.broadcast_to(jnp.sum(jnp.where(lane == sub + i * cols, sums[...], 0.0), axis=1, keepdims=True), shape)
         for i in range(2 * STEPS)]
    none = jnp.zeros(shape, F32)
    one = jnp.ones(shape, F32)
    way, left, made = [one, none, none], [one, none, none, none], [none] * 3
    rz = m[0]
    for k in range(STEPS):
        image = [none] * 4
        for j in range(k + 1):
            image[j + 1] = image[j + 1] + way[j]
            image[j] = image[j] + way[j]
        curve = none
        for i in range(k + 1):
            for j in range(k + 2):
                curve = curve + way[i] * image[j] * m[i + j]
        alpha = rz / curve
        made = [made[j] + alpha * way[j] for j in range(3)]
        left = [left[j] - alpha * image[j] for j in range(4)]
        if k + 1 < STEPS:
            new = none
            for i in range(k + 2):
                for j in range(k + 2):
                    new = new + left[i] * left[j] * m[i + j]
            beta = new / rz
            way = [left[j] + beta * way[j] for j in range(3)]
            rz = new
    for i, x in enumerate(made + left):
        coef[i] = x

    def copies(c):
        return (pltpu.make_async_copy(xs.at[c], out_x.at[c], sem.at[0, c]),
                pltpu.make_async_copy(rs.at[c], out_r.at[c], sem.at[1, c]))

    def column(c, carry):
        x_of = [jnp.broadcast_to(coef[i, pl.ds(c, 1), :], T) for i in range(3)]
        r_of = [jnp.broadcast_to(coef[3 + i, pl.ds(c, 1), :], T) for i in range(4)]
        for a in range(flat // 8):
            rows = pl.ds(8 * a, 8)
            xs[c, rows, :] = x_of[0] * ys[0, c, rows, :] + x_of[1] * ys[1, c, rows, :] + x_of[2] * ys[2, c, rows, :]
            rs[c, rows, :] = (r_of[0] * res[0, c, rows, :] + r_of[1] * res[1, c, rows, :]
                              + r_of[2] * res[2, c, rows, :] + r_of[3] * res[3, c, rows, :])
        for copy in copies(c):
            copy.start()
        return carry

    lax.fori_loop(0, cols, column, 0)
    for c in range(cols):
        for copy in copies(c):
            copy.wait()


def body(loads, material, support, modulus, positions):
    cases, comps, angs, rows, radial = loads.shape
    cols = cases * comps
    na, nh = lax.axis_size("ang"), lax.axis_size("hgt")
    flat = angs * rows
    hbm = pl.BlockSpec(memory_space=pltpu.HBM)
    smem = pl.BlockSpec(memory_space=pltpu.SMEM)
    vmem = pl.BlockSpec(memory_space=pltpu.VMEM)
    v = lambda *shape: pltpu.VMEM((*shape, 128), F32)
    dma = lambda *shape: pltpu.SemaphoreType.DMA(shape)
    res, ys, sums = pl.pallas_call(
        kernel,
        out_shape=(v(STEPS + 1, cols, flat), v(STEPS, cols, flat), v(1)),
        in_specs=[smem, smem, hbm, hbm, hbm],
        out_specs=(vmem, vmem, vmem),
        scratch_shapes=[
            pltpu.VMEM((flat, 128), jnp.int32), pltpu.VMEM((flat, 128), jnp.int32),
            v(flat), v(flat), v(flat), v(flat), v(4, 16), v(4, 16),
            v(cols, flat), v(2, flat),
            v(STEPS, cols + 1, 10, 16),
            v(cols + 1, 16), v(cols + 1, 16), v(4, cols // 2 + 1, 8),
            v(STEPS, cols + 1, 16), v(STEPS, cols + 1, 16), v(STEPS, 4, cols // 2 + 1, 8),
            v(8, 3, 8), v(3, 2, 8, 3, 8),
            v(cols, 32), v(cols, 32), v(STEPS, cols, 32), v(STEPS, cols, 32),
            v(STEPS, cols, 8), v(STEPS, cols, 8),
            v(cols, 2 * STEPS, 8), v(8), v(1, 1), v(na * nh, 1),
            pltpu.SemaphoreType.REGULAR((8,)), dma(GROUPS + 2), dma(STEPS, GROUPS + 1, 8), dma(STEPS, GROUPS + 1, 8),
            dma(STEPS, GROUPS, 4), dma(STEPS, GROUPS, 4), pltpu.SemaphoreType.DMA, pltpu.SemaphoreType.DMA,
        ],
        compiler_params=pltpu.CompilerParams(
            collective_id=0, has_side_effects=True, vmem_limit_bytes=55 * 1000 * 1000),
        name="girder_cg",
    )(modulus, positions, loads.reshape(cols, flat, radial), material.reshape(flat, radial), support.reshape(flat, radial))
    out = jax.ShapeDtypeStruct((cols, flat, radial), F32)
    x, r = pl.pallas_call(
        combine,
        out_shape=(out, out),
        in_specs=[vmem, vmem, vmem],
        out_specs=(hbm, hbm),
        scratch_shapes=[v(2 * STEPS + 1, 16), v(cols, flat), v(cols, flat), dma(2, cols)],
        compiler_params=pltpu.CompilerParams(vmem_limit_bytes=16 * 1024 * 1024),
        name="girder_combine",
    )(sums, res, ys)
    return x.reshape(loads.shape), r.reshape(loads.shape)


def solution(mesh):
    field = P(None, None, "ang", "hgt", None)
    cell = P("ang", "hgt", None)
    return jax.shard_map(body, mesh=mesh, in_specs=(field, cell, cell, P(), P()),
                         out_specs=(field, field), check_vma=False)
```

```python
import functools

import jax
import jax.numpy as jnp
from jax import lax
from jax.experimental import pallas as pl
from jax.experimental.pallas import tpu as pltpu
from jax.sharding import PartitionSpec as P

STEPS = 3
SIGMA = 6.5
SPRING = 20.0
OMEGA = 0.8
LOAD = 3.0
GROUPS = 3
MESH = pl.DeviceIdType.MESH
F32 = jnp.float32
T = (8, 128)
UP, DOWN, RIGHT, LEFT, RU, LU, RD, LD = range(8)
SHIFT = ((0, 1), (0, -1), (1, 0), (-1, 0), (1, 1), (-1, 1), (1, -1), (-1, -1))


def kernel(
    modulus, positions, loads, material, support,
    res, ys, sums,
    mat, sup, weight, spring, diag, kf, kv, iw,
    vf, pe, co, sr, sl, sc, hl, hr, rc, pr, ring,
    fsu, fsd, fu, fd, fl, fr, moments, tsum, row, slots,
    spread, in_sem, dsend, drecv, fsend, frecv, psend, precv,
):
    na, nh = lax.axis_size("ang"), lax.axis_size("hgt")
    me_a, me_h = lax.axis_index("ang"), lax.axis_index("hgt")
    cols = loads.shape[0]
    groups = GROUPS
    per = cols // groups
    pcol = cols
    angs = 32
    sub = lax.broadcasted_iota(jnp.int32, T, 0)
    lane = lax.broadcasted_iota(jnp.int32, T, 1)
    has_up, has_down = me_h < nh - 1, me_h > 0

    def device(da, dh):
        return {"ang": lax.rem(me_a + da + na, na), "hgt": me_h + dh}

    def guarded(dh, body):
        if dh > 0:
            pl.when(has_up)(body)
        elif dh < 0:
            pl.when(has_down)(body)
        else:
            body()

    in_copies = [pltpu.make_async_copy(material, mat, in_sem.at[groups]),
                 pltpu.make_async_copy(support, sup, in_sem.at[groups + 1])]
    for copy in in_copies:
        copy.start()

    def load_copy(g):
        c = pl.ds(g * per, per)
        return pltpu.make_async_copy(loads.at[c], res.at[0, c], in_sem.at[g])

    for g in range(groups):
        load_copy(g).start()

    barrier = pltpu.get_barrier_semaphore()

    def neighbour(da, dh, sem):
        pl.semaphore_signal(sem, inc=1, device_id=device(da, dh), device_id_type=MESH)

    for da, dh in SHIFT:
        guarded(dh, lambda da=da, dh=dh: neighbour(da, dh, barrier))

    rounds = ([(0, 1 << i) for i in range((na // 2 - 1).bit_length())]
              + [(1, 1 << i) for i in range((nh - 1).bit_length())])

    def far(r, body):
        axis, d = rounds[r]
        if axis == 0:
            body(d, 0)
            body(-d, 0)
        else:
            pl.when(me_h + d < nh)(lambda: body(0, d))
            pl.when(me_h - d >= 0)(lambda: body(0, -d))

    def tell(r):
        if r < len(rounds):
            far(r, lambda da, dh: neighbour(da, dh, spread.at[r]))

    def hear(r):
        if r < len(rounds):
            axis, d = rounds[r]
            many = 2 if axis == 0 else (me_h + d < nh).astype(jnp.int32) + (me_h - d >= 0).astype(jnp.int32)
            pl.semaphore_wait(spread.at[r], many)

    def roll(x, shift, axis=0):
        return pltpu.roll(x, shift % x.shape[axis], axis)

    def lanes(v):
        return jnp.where(lane == 0, 0.0, roll(v, 1, 1)) + jnp.where(lane == 127, 0.0, roll(v, -1, 1))

    def quad(ref, j, b, *lead):
        total = None
        for da in range(2):
            for dh in range(2):
                part = ref[(*lead, pl.ds(b * 128 + da * 8 + 2 * j + dh, 8, stride=16), slice(None))]
                total = part if total is None else total + part
        return total

    zero = jnp.zeros(T, F32)

    def clear(row, corners, fine):
        def one(c, carry):
            for k in range(STEPS):
                for j in range(3):
                    for b in range(2):
                        co[k, c, row + j, pl.ds(8 * b, 8), :] = zero
            return carry

        lax.fori_loop(0, cols + 1, one, 0)

        def two(c, carry):
            for k in range(STEPS):
                for i in range(4):
                    fine[k, c, pl.ds(8 * i, 8), :] = zero
            return carry

        lax.fori_loop(0, cols, two, 0)

        def three(c, carry):
            for k in range(STEPS):
                for d in corners:
                    rc[k, d, c] = zero
            return carry

        lax.fori_loop(0, cols // 2 + 1, three, 0)

    def deep(k, slot, first, count, d):
        c = pl.ds(first, count)
        pair = pl.ds(first // 2, (count + 1) // 2)
        if d == UP:
            src, dst = co.at[k, c, pl.ds(4, 3)], co.at[k, c, pl.ds(0, 3)]
        elif d == DOWN:
            src, dst = co.at[k, c, pl.ds(3, 3)], co.at[k, c, pl.ds(7, 3)]
        elif d == RIGHT:
            src, dst = sr.at[c], hl.at[k, c]
        elif d == LEFT:
            src, dst = sl.at[c], hr.at[k, c]
        else:
            src, dst = sc.at[d - 4, pair], rc.at[k, d - 4, pair]
        return pltpu.make_async_remote_copy(
            src_ref=src, dst_ref=dst, send_sem=dsend.at[k, slot, d], recv_sem=drecv.at[k, slot, d],
            device_id=device(*SHIFT[d]), device_id_type=MESH)

    def deep_start(k, slot, first, count):
        for d in (RU, LU, RD, LD, RIGHT, LEFT, UP, DOWN):
            guarded(SHIFT[d][1], lambda d=d: deep(k, slot, first, count, d).start())

    def deep_wait(k, slot, first, count):
        for d in range(8):
            guarded(SHIFT[d][1], lambda d=d: deep(k, slot, first, count, d).wait_send())
            guarded(-SHIFT[d][1], lambda d=d: deep(k, slot, first, count, d).wait_recv())

    def fine(k, g, d):
        c = pl.ds(g * per, per)
        if d == UP:
            src, dst = fsu.at[c], fd.at[k, c]
        elif d == DOWN:
            src, dst = fsd.at[c], fu.at[k, c]
        elif d == RIGHT:
            src, dst = vf.at[c, pl.ds(8 * (angs - 1), 8)], fl.at[k, c]
        else:
            src, dst = vf.at[c, pl.ds(0, 8)], fr.at[k, c]
        return pltpu.make_async_remote_copy(
            src_ref=src, dst_ref=dst, send_sem=fsend.at[k, g, d], recv_sem=frecv.at[k, g, d],
            device_id=device(*SHIFT[d]), device_id_type=MESH)

    def fine_start(k, g):
        for d in (RIGHT, LEFT, UP, DOWN):
            guarded(SHIFT[d][1], lambda d=d: fine(k, g, d).start())

    def fine_wait(k, g):
        for d in range(4):
            guarded(SHIFT[d][1], lambda d=d: fine(k, g, d).wait_send())
            guarded(-SHIFT[d][1], lambda d=d: fine(k, g, d).wait_recv())

    def corner_tiles(k, c):
        low = [co[k, c, 3 + h, pl.ds(0, 8), :] for h in range(4)]
        high = [co[k, c, 3 + h, pl.ds(8, 8), :] for h in range(4)]
        for t in range(2):
            sr[c, pl.ds(8 * t, 8), :] = jnp.where(sub < 4, roll(high[2 * t], 4), high[2 * t + 1])
            sl[c, pl.ds(8 * t, 8), :] = jnp.where(sub < 4, low[2 * t], roll(low[2 * t + 1], 4))
        return (
            jnp.where(sub == 5, roll(high[2], -2), high[3]),
            jnp.where(sub == 2, roll(low[2], 2), low[3]),
            jnp.where(sub == 5, roll(high[1], -2), high[0]),
            jnp.where(sub == 2, roll(low[1], 2), low[0]),
        )

    def merge(d, even, odd):
        if d in (RU, RD):
            return jnp.where(sub < 4, roll(even, 4), odd)
        return jnp.where(sub < 4, even, roll(odd, 4))

    def pack_pair(k, pair):
        even, odd = corner_tiles(k, 2 * pair), corner_tiles(k, 2 * pair + 1)
        for d in (RU, LU, RD, LD):
            sc[d - 4, pair] = merge(d, even[d - 4], odd[d - 4])

    def halo(k, c, pair, parity, h):
        if 0 <= h < 4:
            t = h // 2
            q, p = hr[k, c, pl.ds(8 * t, 8), :], hl[k, c, pl.ds(8 * t, 8), :]
            if h % 2 == 0:
                return jnp.where(sub < 4, q, roll(p, 4))
            return jnp.where(sub < 4, roll(q, 4), p)
        left = rc[k, (RU if h < 0 else RD) - 4, pair]
        right = rc[k, (LU if h < 0 else LD) - 4, pair]
        if parity == 0:
            left = roll(left, 4)
        else:
            right = roll(right, 4)
        if h in (-2, 5):
            left, right = roll(left, 2), roll(right, -2)
        return jnp.where(sub < 4, right, left)

    def ring_row(k, c, pair, parity, h):
        return [co[k, c, 3 + h, pl.ds(0, 8), :], co[k, c, 3 + h, pl.ds(8, 8), :], halo(k, c, pair, parity, h)]

    for copy in in_copies:
        copy.wait()

    def weigh(a, carry):
        rows = pl.ds(pl.multiple_of(a * 8, 8), 8)
        kind = mat[rows, :]
        stiff = zero
        for level in range(modulus.shape[0]):
            stiff = stiff + jnp.where(kind == level, modulus[level], 0.0)
        w = jnp.sqrt(stiff)
        s = sup[rows, :].astype(F32)
        d = SIGMA * w * w + SPRING * s
        weight[rows, :] = w
        spring[rows, :] = s
        diag[rows, :] = d
        kf[rows, :] = OMEGA / d
        return carry

    lax.fori_loop(0, angs, weigh, 0, unroll=4)
    for j in range(4):
        for b in range(2):
            wc = 0.25 * quad(weight, j, b)
            s = 0.25 * quad(spring, j, b)
            kd = OMEGA / (SIGMA * wc * wc + SPRING * s)
            kv[j, pl.ds(8 * b, 8), :] = 0.5 * wc * kd
            iw[j, pl.ds(8 * b, 8), :] = 0.5 / wc
            co[0, pcol, 3 + j, pl.ds(8 * b, 8), :] = wc * wc * kd
    tiles = corner_tiles(0, pcol)
    for d in (RU, LU, RD, LD):
        sc[d - 4, pcol // 2] = merge(d, tiles[d - 4], zero)

    sides = has_up.astype(jnp.int32) + has_down.astype(jnp.int32)
    pl.semaphore_wait(barrier, 2 + 3 * sides)
    tell(0)
    deep_start(0, groups, pcol, 1)

    def restrict(k, c):
        for j in range(4):
            for b in range(2):
                co[k, c, 3 + j, pl.ds(8 * b, 8), :] = kv[j, pl.ds(8 * b, 8), :] * quad(res, j, b, k, c)

    def send_deep(k, g):
        lax.fori_loop(0, per // 2, lambda i, carry: (pack_pair(k, g * (per // 2) + i), carry)[1], 0)
        deep_start(k, g, g * per, per)

    total_angles = na * angs

    def first(g):
        load_copy(g).wait()

        def column(i, carry):
            c = g * per + i
            amount = jnp.where(lax.rem(c, 3) == 2, -LOAD, 0.0)
            spot = jnp.full(T, me_a * angs, jnp.int32) - positions[c // 3]
            for a in range(angs):
                apart = jnp.abs(spot + a)
                near = jnp.minimum(apart, total_angles - apart) < angs
                res[0, c, pl.ds(8 * a, 8), :] += jnp.where(near, amount, 0.0)
            restrict(0, c)
            return carry

        lax.fori_loop(0, per, column, 0)
        send_deep(0, g)

    def coarse_ring():
        deep_wait(0, groups, pcol, 1)
        for h in range(-2, 6):
            row = ring_row(0, pcol, pcol // 2, 0, h)
            for b in range(3):
                pr[h + 2, b] = row[b]

    def sweeps(k, c, pair, parity):
        v0 = {h: ring_row(k, c, pair, parity, h) for h in range(-2, 6)}
        for h in range(-2, 6):
            for b in range(3):
                ring[0, parity, h + 2, b] = v0[h][b]
        outer = {h: [co[k, c, 3 + h, pl.ds(0, 8), :], co[k, c, 3 + h, pl.ds(8, 8), :]] for h in (-3, 6)}
        for sweep in range(3):
            def get(h, b):
                if h in outer:
                    return outer[h][b]
                return ring[sweep, parity, h + 2, b]

            for h in range(-2 + sweep, 6 - sweep):
                edge = h in (-2 + sweep, 5 - sweep)
                me = [get(h, b) for b in range(3)]
                back = [roll(x, 1) for x in me]
                ahead = [roll(x, -1) for x in me]
                for b in range(2 if edge or sweep == 2 else 3):
                    beside = jnp.where(sub == 0, back[b - 1], back[b]) + jnp.where(sub == 7, ahead[(b + 1) % 3], ahead[b])
                    beside = beside + (get(h - 1, b) + get(h + 1, b)) + lanes(me[b])
                    new = (1.0 - OMEGA) * me[b] + ring[0, parity, h + 2, b] + pr[h + 2, b] * beside
                    if sweep < 2:
                        ring[sweep + 1, parity, h + 2, b] = new
                    else:
                        new = new * iw[h, pl.ds(8 * b, 8), :]
                        for da in range(2):
                            for dh in range(2):
                                pe[parity, pl.ds(b * 128 + da * 8 + 2 * h + dh, 8, stride=16), :] = new

    def prolong(k, g, c, parity):
        acc = zero
        for a in range(angs):
            rows = pl.ds(8 * a, 8)
            r = res[k, c, rows, :]
            z = kf[rows, :] * r + pe[parity, rows, :]
            ys[k, c, rows, :] = z
            acc = acc + r * z
            vf[c, rows, :] = weight[rows, :] * z
        moments[c, 2 * k] = acc
        for i in range(4):
            fsu[c, pl.ds(8 * i, 8), :] = vf[c, pl.ds(64 * i + 7, 8, stride=8), :]
            fsd[c, pl.ds(8 * i, 8), :] = vf[c, pl.ds(64 * i, 8, stride=8), :]

    def precondition(k, g):
        deep_wait(k, g, g * per, per)

        def pair_body(i, carry):
            pair = g * (per // 2) + i
            for parity in range(2):
                sweeps(k, 2 * pair + parity, pair, parity)
            for parity in range(2):
                prolong(k, g, 2 * pair + parity, parity)
            return carry

        lax.fori_loop(0, per // 2, pair_body, 0)
        fine_start(k, g)

    def apply_fine(k, g):
        fine_wait(k, g)

        def column(i, carry):
            c = g * per + i
            acc = zero
            before, now = fl[k, c], vf[c, pl.ds(0, 8), :]
            for a in range(angs):
                rows = pl.ds(8 * a, 8)
                after = vf[c, pl.ds(8 * (a + 1), 8), :] if a < angs - 1 else fr[k, c]
                below = jnp.where(sub == 0, fd[k, c, pl.ds(a, 1), :], roll(now, 1))
                above = jnp.where(sub == 7, fu[k, c, pl.ds(a, 1), :], roll(now, -1))
                beside = (before + after) + (below + above) + lanes(now)
                z = ys[k, c, rows, :]
                r = diag[rows, :] * z - weight[rows, :] * beside - res[k, c, rows, :]
                res[k + 1, c, rows, :] = r
                acc = acc + r * z
                before, now = now, after
            moments[c, 2 * k + 1] = acc
            if k + 1 < STEPS:
                restrict(k + 1, c)
            return carry

        lax.fori_loop(0, per, column, 0)
        if k + 1 < STEPS:
            send_deep(k + 1, g)

    def reduce_moments(g):
        for i in range(per):
            c = g * per + i
            rows = zero
            for m in range(2 * STEPS):
                rows = jnp.where(sub == m, jnp.sum(moments[c, m], axis=0, keepdims=True), rows)
            tsum[...] += jnp.where(lane == sub * cols + c, jnp.sum(rows, axis=1, keepdims=True), 0.0)

    def total_moments():
        n, me = na * nh, me_a * nh + me_h
        row[0] = jnp.sum(tsum[...], axis=0, keepdims=True)

        def one(d, carry):
            other = lax.rem(me + d, n)
            pltpu.make_async_remote_copy(
                src_ref=row.at[0], dst_ref=slots.at[me], send_sem=psend, recv_sem=precv,
                device_id={"ang": other // nh, "hgt": lax.rem(other, nh)}, device_id_type=MESH).start()
            return carry

        lax.fori_loop(1, n, one, 0)
        slots[me] = row[0]
        many = slots.at[pl.ds(0, n - 1)]
        pltpu.make_async_copy(many, many, psend).wait()
        pltpu.make_async_copy(many, many, precv).wait()
        parts = [slots[i] for i in range(8)]
        for i in range(8, n):
            parts[i % 8] = parts[i % 8] + slots[i]
        while len(parts) > 1:
            parts = [x + y for x, y in zip(parts[::2], parts[1::2])]
        return parts[0]

    def stage(s, g):
        if s == 0:
            first(g)
        elif s % 2:
            precondition(s // 2, g)
        else:
            apply_fine(s // 2 - 1, g)
            if s == 2 * STEPS:
                reduce_moments(g)

    tsum[...] = zero
    for t in range(2 * STEPS + 1):
        if t == 1:
            pl.when(jnp.logical_not(has_down))(lambda: clear(0, (RU - 4, LU - 4), fd))
            pl.when(jnp.logical_not(has_up))(lambda: clear(7, (RD - 4, LD - 4), fu))
            coarse_ring()
        lax.fori_loop(0, groups, lambda g, carry: (stage(t, g), carry)[1], 0)
        if t >= 1:
            hear(t - 1)
            tell(t)

    sums[...] = total_moments()


def combine(sums, res, ys, out_x, out_r, coef, xs, rs, sem):
    cols, flat, _ = out_x.shape
    shape = (16, 128)
    sub = lax.broadcasted_iota(jnp.int32, shape, 0)
    lane = lax.broadcasted_iota(jnp.int32, shape, 1)
    m = [jnp.broadcast_to(jnp.sum(jnp.where(lane == sub + i * cols, sums[...], 0.0), axis=1, keepdims=True), shape)
         for i in range(2 * STEPS)]
    none = jnp.zeros(shape, F32)
    one = jnp.ones(shape, F32)
    way, left, made = [one, none, none], [one, none, none, none], [none] * 3
    rz = m[0]
    for k in range(STEPS):
        image = [none] * 4
        for j in range(k + 1):
            image[j + 1] = image[j + 1] + way[j]
            image[j] = image[j] + way[j]
        curve = none
        for i in range(k + 1):
            for j in range(k + 2):
                curve = curve + way[i] * image[j] * m[i + j]
        alpha = rz / curve
        made = [made[j] + alpha * way[j] for j in range(3)]
        left = [left[j] - alpha * image[j] for j in range(4)]
        if k + 1 < STEPS:
            new = none
            for i in range(k + 2):
                for j in range(k + 2):
                    new = new + left[i] * left[j] * m[i + j]
            beta = new / rz
            way = [left[j] + beta * way[j] for j in range(3)]
            rz = new
    for i, x in enumerate(made + left):
        coef[i] = x

    def copies(c):
        return (pltpu.make_async_copy(xs.at[c], out_x.at[c], sem.at[0, c]),
                pltpu.make_async_copy(rs.at[c], out_r.at[c], sem.at[1, c]))

    def column(c, carry):
        x_of = [jnp.broadcast_to(coef[i, pl.ds(c, 1), :], T) for i in range(3)]
        r_of = [jnp.broadcast_to(coef[3 + i, pl.ds(c, 1), :], T) for i in range(4)]
        for a in range(flat // 8):
            rows = pl.ds(8 * a, 8)
            xs[c, rows, :] = x_of[0] * ys[0, c, rows, :] + x_of[1] * ys[1, c, rows, :] + x_of[2] * ys[2, c, rows, :]
            rs[c, rows, :] = (r_of[0] * res[0, c, rows, :] + r_of[1] * res[1, c, rows, :]
                              + r_of[2] * res[2, c, rows, :] + r_of[3] * res[3, c, rows, :])
        for copy in copies(c):
            copy.start()
        return carry

    lax.fori_loop(0, cols, column, 0)
    for c in range(cols):
        for copy in copies(c):
            copy.wait()


def body(loads, material, support, modulus, positions):
    cases, comps, angs, rows, radial = loads.shape
    cols = cases * comps
    na, nh = lax.axis_size("ang"), lax.axis_size("hgt")
    flat = angs * rows
    hbm = pl.BlockSpec(memory_space=pltpu.HBM)
    smem = pl.BlockSpec(memory_space=pltpu.SMEM)
    vmem = pl.BlockSpec(memory_space=pltpu.VMEM)
    v = lambda *shape: pltpu.VMEM((*shape, 128), F32)
    dma = lambda *shape: pltpu.SemaphoreType.DMA(shape)
    res, ys, sums = pl.pallas_call(
        kernel,
        out_shape=(v(STEPS + 1, cols, flat), v(STEPS, cols, flat), v(1)),
        in_specs=[smem, smem, hbm, hbm, hbm],
        out_specs=(vmem, vmem, vmem),
        scratch_shapes=[
            pltpu.VMEM((flat, 128), jnp.int32), pltpu.VMEM((flat, 128), jnp.int32),
            v(flat), v(flat), v(flat), v(flat), v(4, 16), v(4, 16),
            v(cols, flat), v(2, flat),
            v(STEPS, cols + 1, 10, 16),
            v(cols + 1, 16), v(cols + 1, 16), v(4, cols // 2 + 1, 8),
            v(STEPS, cols + 1, 16), v(STEPS, cols + 1, 16), v(STEPS, 4, cols // 2 + 1, 8),
            v(8, 3, 8), v(3, 2, 8, 3, 8),
            v(cols, 32), v(cols, 32), v(STEPS, cols, 32), v(STEPS, cols, 32),
            v(STEPS, cols, 8), v(STEPS, cols, 8),
            v(cols, 2 * STEPS, 8), v(8), v(1, 1), v(na * nh, 1),
            pltpu.SemaphoreType.REGULAR((8,)), dma(GROUPS + 2), dma(STEPS, GROUPS + 1, 8), dma(STEPS, GROUPS + 1, 8),
            dma(STEPS, GROUPS, 4), dma(STEPS, GROUPS, 4), pltpu.SemaphoreType.DMA, pltpu.SemaphoreType.DMA,
        ],
        compiler_params=pltpu.CompilerParams(
            collective_id=0, has_side_effects=True, vmem_limit_bytes=55 * 1000 * 1000),
        name="girder_cg",
    )(modulus, positions, loads.reshape(cols, flat, radial), material.reshape(flat, radial), support.reshape(flat, radial))
    out = jax.ShapeDtypeStruct((cols, flat, radial), F32)
    x, r = pl.pallas_call(
        combine,
        out_shape=(out, out),
        in_specs=[vmem, vmem, vmem],
        out_specs=(hbm, hbm),
        scratch_shapes=[v(2 * STEPS + 1, 16), v(cols, flat), v(cols, flat), dma(2, cols)],
        compiler_params=pltpu.CompilerParams(vmem_limit_bytes=16 * 1024 * 1024),
        name="girder_combine",
    )(sums, res, ys)
    return x.reshape(loads.shape), r.reshape(loads.shape)


def solution(mesh):
    field = P(None, None, "ang", "hgt", None)
    cell = P("ang", "hgt", None)
    return jax.shard_map(body, mesh=mesh, in_specs=(field, cell, cell, P(), P()),
                         out_specs=(field, field), check_vma=False)
```

```python
import functools

import jax
import jax.numpy as jnp
from jax import lax
from jax.experimental import pallas as pl
from jax.experimental.pallas import tpu as pltpu
from jax.sharding import PartitionSpec as P

STEPS = 3
SIGMA = 6.5
SPRING = 20.0
OMEGA = 0.8
LOAD = 3.0
GROUPS = 3
MESH = pl.DeviceIdType.MESH
F32 = jnp.float32
T = (8, 128)
UP, DOWN, RIGHT, LEFT, RU, LU, RD, LD = range(8)
SHIFT = ((0, 1), (0, -1), (1, 0), (-1, 0), (1, 1), (-1, 1), (1, -1), (-1, -1))


def kernel(
    modulus, positions, loads, material, support,
    res, ys, sums,
    mat, sup, weight, spring, diag, kf, kv, iw,
    vf, pe, co, sr, sl, sc, hl, hr, rc, pr, ring,
    fsu, fsd, fu, fd, fl, fr, moments, tsum, row, slots,
    spread, in_sem, dsend, drecv, fsend, frecv, psend, precv,
):
    na, nh = lax.axis_size("ang"), lax.axis_size("hgt")
    me_a, me_h = lax.axis_index("ang"), lax.axis_index("hgt")
    cols = loads.shape[0]
    groups = GROUPS
    per = cols // groups
    pcol = cols
    angs = 32
    sub = lax.broadcasted_iota(jnp.int32, T, 0)
    lane = lax.broadcasted_iota(jnp.int32, T, 1)
    has_up, has_down = me_h < nh - 1, me_h > 0

    def device(da, dh):
        return {"ang": lax.rem(me_a + da + na, na), "hgt": me_h + dh}

    def guarded(dh, body):
        if dh > 0:
            pl.when(has_up)(body)
        elif dh < 0:
            pl.when(has_down)(body)
        else:
            body()

    in_copies = [pltpu.make_async_copy(material, mat, in_sem.at[groups]),
                 pltpu.make_async_copy(support, sup, in_sem.at[groups + 1])]
    for copy in in_copies:
        copy.start()

    def load_copy(g):
        c = pl.ds(g * per, per)
        return pltpu.make_async_copy(loads.at[c], res.at[0, c], in_sem.at[g])

    for g in range(groups):
        load_copy(g).start()

    barrier = pltpu.get_barrier_semaphore()

    def neighbour(da, dh, sem):
        pl.semaphore_signal(sem, inc=1, device_id=device(da, dh), device_id_type=MESH)

    for da, dh in SHIFT:
        guarded(dh, lambda da=da, dh=dh: neighbour(da, dh, barrier))

    rounds = ([(0, 1 << i) for i in range((na // 2 - 1).bit_length())]
              + [(1, 1 << i) for i in range((nh - 1).bit_length())])

    def far(r, body):
        axis, d = rounds[r]
        if axis == 0:
            body(d, 0)
            body(-d, 0)
        else:
            pl.when(me_h + d < nh)(lambda: body(0, d))
            pl.when(me_h - d >= 0)(lambda: body(0, -d))

    def tell(r):
        if r < len(rounds):
            far(r, lambda da, dh: neighbour(da, dh, spread.at[r]))

    def hear(r):
        if r < len(rounds):
            axis, d = rounds[r]
            many = 2 if axis == 0 else (me_h + d < nh).astype(jnp.int32) + (me_h - d >= 0).astype(jnp.int32)
            pl.semaphore_wait(spread.at[r], many)

    def roll(x, shift, axis=0):
        return pltpu.roll(x, shift % x.shape[axis], axis)

    def lanes(v):
        return jnp.where(lane == 0, 0.0, roll(v, 1, 1)) + jnp.where(lane == 127, 0.0, roll(v, -1, 1))

    def quad(ref, j, b, *lead):
        total = None
        for da in range(2):
            for dh in range(2):
                part = ref[(*lead, pl.ds(b * 128 + da * 8 + 2 * j + dh, 8, stride=16), slice(None))]
                total = part if total is None else total + part
        return total

    zero = jnp.zeros(T, F32)

    def clear(row, corners, fine):
        def one(c, carry):
            for k in range(STEPS):
                for j in range(3):
                    for b in range(2):
                        co[k, c, row + j, pl.ds(8 * b, 8), :] = zero
            return carry

        lax.fori_loop(0, cols + 1, one, 0)

        def two(c, carry):
            for k in range(STEPS):
                for i in range(4):
                    fine[k, c, pl.ds(8 * i, 8), :] = zero
            return carry

        lax.fori_loop(0, cols, two, 0)

        def three(c, carry):
            for k in range(STEPS):
                for d in corners:
                    rc[k, d, c] = zero
            return carry

        lax.fori_loop(0, cols // 2 + 1, three, 0)

    def deep(k, slot, first, count, d):
        c = pl.ds(first, count)
        pair = pl.ds(first // 2, (count + 1) // 2)
        if d == UP:
            src, dst = co.at[k, c, pl.ds(4, 3)], co.at[k, c, pl.ds(0, 3)]
        elif d == DOWN:
            src, dst = co.at[k, c, pl.ds(3, 3)], co.at[k, c, pl.ds(7, 3)]
        elif d == RIGHT:
            src, dst = sr.at[c], hl.at[k, c]
        elif d == LEFT:
            src, dst = sl.at[c], hr.at[k, c]
        else:
            src, dst = sc.at[d - 4, pair], rc.at[k, d - 4, pair]
        return pltpu.make_async_remote_copy(
            src_ref=src, dst_ref=dst, send_sem=dsend.at[k, slot, d], recv_sem=drecv.at[k, slot, d],
            device_id=device(*SHIFT[d]), device_id_type=MESH)

    def deep_start(k, slot, first, count):
        for d in (RU, LU, RD, LD, RIGHT, LEFT, UP, DOWN):
            guarded(SHIFT[d][1], lambda d=d: deep(k, slot, first, count, d).start())

    def deep_wait(k, slot, first, count):
        for d in range(8):
            guarded(SHIFT[d][1], lambda d=d: deep(k, slot, first, count, d).wait_send())
            guarded(-SHIFT[d][1], lambda d=d: deep(k, slot, first, count, d).wait_recv())

    half = angs // 2

    def fine_parts(d, part):
        if part is None:
            return pl.ds(0, angs)
        if d == UP:
            return pl.ds(half, half) if part == 0 else pl.ds(0, half)
        if d == DOWN:
            return pl.ds(0, half) if part == 0 else pl.ds(half, half)
        return None if (d == LEFT) != (part == 0) else pl.ds(0, angs)

    def fine(k, g, d, part):
        c = pl.ds(g * per, per)
        rows = fine_parts(d, part)
        if d == UP:
            src, dst = fsu.at[c, rows], fd.at[k, c, rows]
        elif d == DOWN:
            src, dst = fsd.at[c, rows], fu.at[k, c, rows]
        elif d == RIGHT:
            src, dst = vf.at[c, pl.ds(8 * (angs - 1), 8)], fl.at[k, c]
        else:
            src, dst = vf.at[c, pl.ds(0, 8)], fr.at[k, c]
        i = d + 4 if part == 1 else d
        return pltpu.make_async_remote_copy(
            src_ref=src, dst_ref=dst, send_sem=fsend.at[k, g, i], recv_sem=frecv.at[k, g, i],
            device_id=device(*SHIFT[d]), device_id_type=MESH)

    def fine_start(k, g, part):
        for d in (RIGHT, LEFT, UP, DOWN):
            if fine_parts(d, part) is not None:
                guarded(SHIFT[d][1], lambda d=d: fine(k, g, d, part).start())

    def fine_wait(k, g, part):
        for d in range(4):
            if fine_parts(d, part) is not None:
                guarded(SHIFT[d][1], lambda d=d: fine(k, g, d, part).wait_send())
                guarded(-SHIFT[d][1], lambda d=d: fine(k, g, d, part).wait_recv())

    def corner_tiles(k, c):
        low = [co[k, c, 3 + h, pl.ds(0, 8), :] for h in range(4)]
        high = [co[k, c, 3 + h, pl.ds(8, 8), :] for h in range(4)]
        for t in range(2):
            sr[c, pl.ds(8 * t, 8), :] = jnp.where(sub < 4, roll(high[2 * t], 4), high[2 * t + 1])
            sl[c, pl.ds(8 * t, 8), :] = jnp.where(sub < 4, low[2 * t], roll(low[2 * t + 1], 4))
        return (
            jnp.where(sub == 5, roll(high[2], -2), high[3]),
            jnp.where(sub == 2, roll(low[2], 2), low[3]),
            jnp.where(sub == 5, roll(high[1], -2), high[0]),
            jnp.where(sub == 2, roll(low[1], 2), low[0]),
        )

    def merge(d, even, odd):
        if d in (RU, RD):
            return jnp.where(sub < 4, roll(even, 4), odd)
        return jnp.where(sub < 4, even, roll(odd, 4))

    def pack_pair(k, pair):
        even, odd = corner_tiles(k, 2 * pair), corner_tiles(k, 2 * pair + 1)
        for d in (RU, LU, RD, LD):
            sc[d - 4, pair] = merge(d, even[d - 4], odd[d - 4])

    def halo(k, c, pair, parity, h):
        if 0 <= h < 4:
            t = h // 2
            q, p = hr[k, c, pl.ds(8 * t, 8), :], hl[k, c, pl.ds(8 * t, 8), :]
            if h % 2 == 0:
                return jnp.where(sub < 4, q, roll(p, 4))
            return jnp.where(sub < 4, roll(q, 4), p)
        left = rc[k, (RU if h < 0 else RD) - 4, pair]
        right = rc[k, (LU if h < 0 else LD) - 4, pair]
        if parity == 0:
            left = roll(left, 4)
        else:
            right = roll(right, 4)
        if h in (-2, 5):
            left, right = roll(left, 2), roll(right, -2)
        return jnp.where(sub < 4, right, left)

    def ring_row(k, c, pair, parity, h):
        return [co[k, c, 3 + h, pl.ds(0, 8), :], co[k, c, 3 + h, pl.ds(8, 8), :], halo(k, c, pair, parity, h)]

    for copy in in_copies:
        copy.wait()

    def weigh(a, carry):
        rows = pl.ds(pl.multiple_of(a * 8, 8), 8)
        kind = mat[rows, :]
        stiff = zero
        for level in range(modulus.shape[0]):
            stiff = stiff + jnp.where(kind == level, modulus[level], 0.0)
        w = jnp.sqrt(stiff)
        s = sup[rows, :].astype(F32)
        d = SIGMA * w * w + SPRING * s
        weight[rows, :] = w
        spring[rows, :] = s
        diag[rows, :] = d
        kf[rows, :] = OMEGA / d
        return carry

    lax.fori_loop(0, angs, weigh, 0, unroll=4)
    for j in range(4):
        for b in range(2):
            wc = 0.25 * quad(weight, j, b)
            s = 0.25 * quad(spring, j, b)
            kd = OMEGA / (SIGMA * wc * wc + SPRING * s)
            kv[j, pl.ds(8 * b, 8), :] = 0.5 * wc * kd
            iw[j, pl.ds(8 * b, 8), :] = 0.5 / wc
            co[0, pcol, 3 + j, pl.ds(8 * b, 8), :] = wc * wc * kd
    tiles = corner_tiles(0, pcol)
    for d in (RU, LU, RD, LD):
        sc[d - 4, pcol // 2] = merge(d, tiles[d - 4], zero)

    sides = has_up.astype(jnp.int32) + has_down.astype(jnp.int32)
    pl.semaphore_wait(barrier, 2 + 3 * sides)
    tell(0)
    deep_start(0, groups, pcol, 1)

    def restrict(k, c):
        for j in range(4):
            for b in range(2):
                co[k, c, 3 + j, pl.ds(8 * b, 8), :] = kv[j, pl.ds(8 * b, 8), :] * quad(res, j, b, k, c)

    def send_deep(k, g):
        lax.fori_loop(0, per // 2, lambda i, carry: (pack_pair(k, g * (per // 2) + i), carry)[1], 0)
        deep_start(k, g, g * per, per)

    total_angles = na * angs

    def first(g):
        load_copy(g).wait()

        def column(i, carry):
            c = g * per + i
            amount = jnp.where(lax.rem(c, 3) == 2, -LOAD, 0.0)
            spot = jnp.full(T, me_a * angs, jnp.int32) - positions[c // 3]
            for a in range(angs):
                apart = jnp.abs(spot + a)
                near = jnp.minimum(apart, total_angles - apart) < angs
                res[0, c, pl.ds(8 * a, 8), :] += jnp.where(near, amount, 0.0)
            restrict(0, c)
            return carry

        lax.fori_loop(0, per, column, 0)
        send_deep(0, g)

    def coarse_ring():
        deep_wait(0, groups, pcol, 1)
        for h in range(-2, 6):
            row = ring_row(0, pcol, pcol // 2, 0, h)
            for b in range(3):
                pr[h + 2, b] = row[b]

    def sweeps(k, c, pair, parity):
        v0 = {h: ring_row(k, c, pair, parity, h) for h in range(-2, 6)}
        for h in range(-2, 6):
            for b in range(3):
                ring[0, parity, h + 2, b] = v0[h][b]
        outer = {h: [co[k, c, 3 + h, pl.ds(0, 8), :], co[k, c, 3 + h, pl.ds(8, 8), :]] for h in (-3, 6)}
        for sweep in range(3):
            def get(h, b):
                if h in outer:
                    return outer[h][b]
                return ring[sweep, parity, h + 2, b]

            for h in range(-2 + sweep, 6 - sweep):
                edge = h in (-2 + sweep, 5 - sweep)
                me = [get(h, b) for b in range(3)]
                back = [roll(x, 1) for x in me]
                ahead = [roll(x, -1) for x in me]
                for b in range(2 if edge or sweep == 2 else 3):
                    beside = jnp.where(sub == 0, back[b - 1], back[b]) + jnp.where(sub == 7, ahead[(b + 1) % 3], ahead[b])
                    beside = beside + (get(h - 1, b) + get(h + 1, b)) + lanes(me[b])
                    new = (1.0 - OMEGA) * me[b] + ring[0, parity, h + 2, b] + pr[h + 2, b] * beside
                    if sweep < 2:
                        ring[sweep + 1, parity, h + 2, b] = new
                    else:
                        new = new * iw[h, pl.ds(8 * b, 8), :]
                        for da in range(2):
                            for dh in range(2):
                                pe[parity, pl.ds(b * 128 + da * 8 + 2 * h + dh, 8, stride=16), :] = new

    def prolong(k, g, c, parity):
        last = k == STEPS - 1
        acc, square, edges, before = zero, zero, zero, None
        for a in range(angs):
            rows = pl.ds(8 * a, 8)
            r = res[k, c, rows, :]
            z = kf[rows, :] * r + pe[parity, rows, :]
            ys[k, c, rows, :] = z
            acc = acc + r * z
            v = weight[rows, :] * z
            vf[c, rows, :] = v
            if last:
                ahead = jnp.where(sub == 7, 0.0, roll(v, -1)) + jnp.where(lane == 127, 0.0, roll(v, -1, 1))
                square = square + diag[rows, :] * z * z
                edges = edges + v * (ahead if a == 0 else ahead + before)
                before = v
        moments[c, 2 * k] = acc
        if last:
            moments[c, 2 * k + 1] = square - 2.0 * edges - acc
        for i in range(4):
            fsu[c, pl.ds(8 * i, 8), :] = vf[c, pl.ds(64 * i + 7, 8, stride=8), :]
            fsd[c, pl.ds(8 * i, 8), :] = vf[c, pl.ds(64 * i, 8, stride=8), :]

    def precondition(k, g):
        deep_wait(k, g, g * per, per)

        def pair_body(i, carry):
            pair = g * (per // 2) + i
            for parity in range(2):
                sweeps(k, 2 * pair + parity, pair, parity)
            for parity in range(2):
                prolong(k, g, 2 * pair + parity, parity)
            return carry

        lax.fori_loop(0, per // 2, pair_body, 0)
        fine_start(k, g, None if k < STEPS - 1 else 0)

    def apply_fine(k, g):
        fine_wait(k, g, None if k < STEPS - 1 else 1)

        def column(i, carry):
            c = g * per + i
            acc = zero
            before, now = fl[k, c], vf[c, pl.ds(0, 8), :]
            for a in range(angs):
                rows = pl.ds(8 * a, 8)
                after = vf[c, pl.ds(8 * (a + 1), 8), :] if a < angs - 1 else fr[k, c]
                below = jnp.where(sub == 0, fd[k, c, pl.ds(a, 1), :], roll(now, 1))
                above = jnp.where(sub == 7, fu[k, c, pl.ds(a, 1), :], roll(now, -1))
                beside = (before + after) + (below + above) + lanes(now)
                z = ys[k, c, rows, :]
                r = diag[rows, :] * z - weight[rows, :] * beside - res[k, c, rows, :]
                res[k + 1, c, rows, :] = r
                acc = acc + r * z
                before, now = now, after
            if k + 1 < STEPS:
                moments[c, 2 * k + 1] = acc
                restrict(k + 1, c)
            return carry

        lax.fori_loop(0, per, column, 0)
        if k + 1 < STEPS:
            send_deep(k + 1, g)

    def reduce_moments(g):
        for i in range(per):
            c = g * per + i
            rows = zero
            for m in range(2 * STEPS):
                rows = jnp.where(sub == m, jnp.sum(moments[c, m], axis=0, keepdims=True), rows)
            tsum[...] += jnp.where(lane == sub * cols + c, jnp.sum(rows, axis=1, keepdims=True), 0.0)

    def total_moments():
        n, me = na * nh, me_a * nh + me_h
        row[0] = jnp.sum(tsum[...], axis=0, keepdims=True)

        def one(d, carry):
            other = lax.rem(me + d, n)
            pltpu.make_async_remote_copy(
                src_ref=row.at[0], dst_ref=slots.at[me], send_sem=psend, recv_sem=precv,
                device_id={"ang": other // nh, "hgt": lax.rem(other, nh)}, device_id_type=MESH).start()
            return carry

        lax.fori_loop(1, n, one, 0)
        slots[me] = row[0]
        lax.fori_loop(0, groups, lambda g, carry: (apply_fine(STEPS - 1, g), carry)[1], 0)
        many = slots.at[pl.ds(0, n - 1)]
        pltpu.make_async_copy(many, many, psend).wait()
        pltpu.make_async_copy(many, many, precv).wait()
        parts = [slots[i] for i in range(8)]
        for i in range(8, n):
            parts[i % 8] = parts[i % 8] + slots[i]
        while len(parts) > 1:
            parts = [x + y for x, y in zip(parts[::2], parts[1::2])]
        return parts[0]

    def outer_edges(g):
        k = STEPS - 1
        fine_wait(k, g, 0)
        for i in range(per):
            c = g * per + i
            edges = vf[c, pl.ds(8 * (angs - 1), 8), :] * fr[k, c]
            for at in range(0, half, 8):
                low, high = pl.ds(at, 8), pl.ds(half + at, 8)
                edges = edges + fsu[c, low, :] * fu[k, c, low, :] + fsd[c, high, :] * fd[k, c, high, :]
            moments[c, 2 * k + 1] = moments[c, 2 * k + 1] - 2.0 * edges

    def stage(s, g):
        if s == 0:
            first(g)
        elif s % 2:
            precondition(s // 2, g)
        elif s < 2 * STEPS:
            apply_fine(s // 2 - 1, g)
        else:
            outer_edges(g)
            reduce_moments(g)

    tsum[...] = zero
    for t in range(2 * STEPS + 1):
        if t == 1:
            pl.when(jnp.logical_not(has_down))(lambda: clear(0, (RU - 4, LU - 4), fd))
            pl.when(jnp.logical_not(has_up))(lambda: clear(7, (RD - 4, LD - 4), fu))
            coarse_ring()
        lax.fori_loop(0, groups, lambda g, carry: (stage(t, g), carry)[1], 0)
        if t >= 1:
            hear(t - 1)
            tell(t)
        if t == 2 * STEPS - 1:
            lax.fori_loop(0, groups, lambda g, carry: (fine_start(STEPS - 1, g, 1), carry)[1], 0)

    sums[...] = total_moments()


def combine(sums, res, ys, out_x, out_r, coef, xs, rs, sem):
    cols, flat, _ = out_x.shape
    shape = (16, 128)
    sub = lax.broadcasted_iota(jnp.int32, shape, 0)
    lane = lax.broadcasted_iota(jnp.int32, shape, 1)
    m = [jnp.broadcast_to(jnp.sum(jnp.where(lane == sub + i * cols, sums[...], 0.0), axis=1, keepdims=True), shape)
         for i in range(2 * STEPS)]
    none = jnp.zeros(shape, F32)
    one = jnp.ones(shape, F32)
    way, left, made = [one, none, none], [one, none, none, none], [none] * 3
    rz = m[0]
    for k in range(STEPS):
        image = [none] * 4
        for j in range(k + 1):
            image[j + 1] = image[j + 1] + way[j]
            image[j] = image[j] + way[j]
        curve = none
        for i in range(k + 1):
            for j in range(k + 2):
                curve = curve + way[i] * image[j] * m[i + j]
        alpha = rz / curve
        made = [made[j] + alpha * way[j] for j in range(3)]
        left = [left[j] - alpha * image[j] for j in range(4)]
        if k + 1 < STEPS:
            new = none
            for i in range(k + 2):
                for j in range(k + 2):
                    new = new + left[i] * left[j] * m[i + j]
            beta = new / rz
            way = [left[j] + beta * way[j] for j in range(3)]
            rz = new
    for i, x in enumerate(made + left):
        coef[i] = x

    def copies(c):
        return (pltpu.make_async_copy(xs.at[c], out_x.at[c], sem.at[0, c]),
                pltpu.make_async_copy(rs.at[c], out_r.at[c], sem.at[1, c]))

    def column(c, carry):
        x_of = [jnp.broadcast_to(coef[i, pl.ds(c, 1), :], T) for i in range(3)]
        r_of = [jnp.broadcast_to(coef[3 + i, pl.ds(c, 1), :], T) for i in range(4)]
        for a in range(flat // 8):
            rows = pl.ds(8 * a, 8)
            xs[c, rows, :] = x_of[0] * ys[0, c, rows, :] + x_of[1] * ys[1, c, rows, :] + x_of[2] * ys[2, c, rows, :]
            rs[c, rows, :] = (r_of[0] * res[0, c, rows, :] + r_of[1] * res[1, c, rows, :]
                              + r_of[2] * res[2, c, rows, :] + r_of[3] * res[3, c, rows, :])
        for copy in copies(c):
            copy.start()
        return carry

    lax.fori_loop(0, cols, column, 0)
    for c in range(cols):
        for copy in copies(c):
            copy.wait()


def body(loads, material, support, modulus, positions):
    cases, comps, angs, rows, radial = loads.shape
    cols = cases * comps
    na, nh = lax.axis_size("ang"), lax.axis_size("hgt")
    flat = angs * rows
    hbm = pl.BlockSpec(memory_space=pltpu.HBM)
    smem = pl.BlockSpec(memory_space=pltpu.SMEM)
    vmem = pl.BlockSpec(memory_space=pltpu.VMEM)
    v = lambda *shape: pltpu.VMEM((*shape, 128), F32)
    dma = lambda *shape: pltpu.SemaphoreType.DMA(shape)
    res, ys, sums = pl.pallas_call(
        kernel,
        out_shape=(v(STEPS + 1, cols, flat), v(STEPS, cols, flat), v(1)),
        in_specs=[smem, smem, hbm, hbm, hbm],
        out_specs=(vmem, vmem, vmem),
        scratch_shapes=[
            pltpu.VMEM((flat, 128), jnp.int32), pltpu.VMEM((flat, 128), jnp.int32),
            v(flat), v(flat), v(flat), v(flat), v(4, 16), v(4, 16),
            v(cols, flat), v(2, flat),
            v(STEPS, cols + 1, 10, 16),
            v(cols + 1, 16), v(cols + 1, 16), v(4, cols // 2 + 1, 8),
            v(STEPS, cols + 1, 16), v(STEPS, cols + 1, 16), v(STEPS, 4, cols // 2 + 1, 8),
            v(8, 3, 8), v(3, 2, 8, 3, 8),
            v(cols, 32), v(cols, 32), v(STEPS, cols, 32), v(STEPS, cols, 32),
            v(STEPS, cols, 8), v(STEPS, cols, 8),
            v(cols, 2 * STEPS, 8), v(8), v(1, 1), v(na * nh, 1),
            pltpu.SemaphoreType.REGULAR((8,)), dma(GROUPS + 2), dma(STEPS, GROUPS + 1, 8), dma(STEPS, GROUPS + 1, 8),
            dma(STEPS, GROUPS, 8), dma(STEPS, GROUPS, 8), pltpu.SemaphoreType.DMA, pltpu.SemaphoreType.DMA,
        ],
        compiler_params=pltpu.CompilerParams(
            collective_id=0, has_side_effects=True, vmem_limit_bytes=55 * 1000 * 1000),
        name="girder_cg",
    )(modulus, positions, loads.reshape(cols, flat, radial), material.reshape(flat, radial), support.reshape(flat, radial))
    out = jax.ShapeDtypeStruct((cols, flat, radial), F32)
    x, r = pl.pallas_call(
        combine,
        out_shape=(out, out),
        in_specs=[vmem, vmem, vmem],
        out_specs=(hbm, hbm),
        scratch_shapes=[v(2 * STEPS + 1, 16), v(cols, flat), v(cols, flat), dma(2, cols)],
        compiler_params=pltpu.CompilerParams(vmem_limit_bytes=16 * 1024 * 1024),
        name="girder_combine",
    )(sums, res, ys)
    return x.reshape(loads.shape), r.reshape(loads.shape)


def solution(mesh):
    field = P(None, None, "ang", "hgt", None)
    cell = P("ang", "hgt", None)
    return jax.shard_map(body, mesh=mesh, in_specs=(field, cell, cell, P(), P()),
                         out_specs=(field, field), check_vma=False)
```

```python
import functools

import jax
import jax.numpy as jnp
from jax import lax
from jax.experimental import pallas as pl
from jax.experimental.pallas import tpu as pltpu
from jax.sharding import PartitionSpec as P

STEPS = 3
SIGMA = 6.5
SPRING = 20.0
OMEGA = 0.8
LOAD = 3.0
GROUPS = 3
MESH = pl.DeviceIdType.MESH
F32 = jnp.float32
T = (8, 128)
UP, DOWN, RIGHT, LEFT, RU, LU, RD, LD = range(8)
SHIFT = ((0, 1), (0, -1), (1, 0), (-1, 0), (1, 1), (-1, 1), (1, -1), (-1, -1))


def kernel(
    modulus, positions, loads, material, support,
    res, ys, sums,
    mat, sup, weight, spring, diag, kf, kv, iw,
    vf, pe, co, sr, sl, sc, hl, hr, rc, pr, ring,
    fsu, fsd, fu, fd, fl, fr, moments, tsum, row, slots,
    spread, in_sem, dsend, drecv, fsend, frecv, psend, precv,
):
    na, nh = lax.axis_size("ang"), lax.axis_size("hgt")
    me_a, me_h = lax.axis_index("ang"), lax.axis_index("hgt")
    cols = loads.shape[0]
    groups = GROUPS
    per = cols // groups
    pcol = cols
    angs = 32
    sub = lax.broadcasted_iota(jnp.int32, T, 0)
    lane = lax.broadcasted_iota(jnp.int32, T, 1)
    has_up, has_down = me_h < nh - 1, me_h > 0

    def device(da, dh):
        return {"ang": lax.rem(me_a + da + na, na), "hgt": me_h + dh}

    def guarded(dh, body):
        if dh > 0:
            pl.when(has_up)(body)
        elif dh < 0:
            pl.when(has_down)(body)
        else:
            body()

    in_copies = [pltpu.make_async_copy(material, mat, in_sem.at[groups]),
                 pltpu.make_async_copy(support, sup, in_sem.at[groups + 1])]
    for copy in in_copies:
        copy.start()

    def load_copy(g):
        c = pl.ds(g * per, per)
        return pltpu.make_async_copy(loads.at[c], res.at[0, c], in_sem.at[g])

    for g in range(groups):
        load_copy(g).start()

    barrier = pltpu.get_barrier_semaphore()

    def neighbour(da, dh, sem):
        pl.semaphore_signal(sem, inc=1, device_id=device(da, dh), device_id_type=MESH)

    for da, dh in SHIFT:
        guarded(dh, lambda da=da, dh=dh: neighbour(da, dh, barrier))

    rounds = ([(0, 1 << i) for i in range((na // 2 - 1).bit_length())]
              + [(1, 1 << i) for i in range((nh - 1).bit_length())])

    def far(r, body):
        axis, d = rounds[r]
        if axis == 0:
            body(d, 0)
            body(-d, 0)
        else:
            pl.when(me_h + d < nh)(lambda: body(0, d))
            pl.when(me_h - d >= 0)(lambda: body(0, -d))

    def tell(r):
        if r < len(rounds):
            far(r, lambda da, dh: neighbour(da, dh, spread.at[r]))

    def hear(r):
        if r < len(rounds):
            axis, d = rounds[r]
            many = 2 if axis == 0 else (me_h + d < nh).astype(jnp.int32) + (me_h - d >= 0).astype(jnp.int32)
            pl.semaphore_wait(spread.at[r], many)

    def roll(x, shift, axis=0):
        return pltpu.roll(x, shift % x.shape[axis], axis)

    def lanes(v):
        return jnp.where(lane == 0, 0.0, roll(v, 1, 1)) + jnp.where(lane == 127, 0.0, roll(v, -1, 1))

    def quad(ref, j, b, *lead):
        total = None
        for da in range(2):
            for dh in range(2):
                part = ref[(*lead, pl.ds(b * 128 + da * 8 + 2 * j + dh, 8, stride=16), slice(None))]
                total = part if total is None else total + part
        return total

    zero = jnp.zeros(T, F32)

    def clear(row, corners, fine):
        def one(c, carry):
            for k in range(STEPS):
                for j in range(3):
                    for b in range(2):
                        co[k, c, row + j, pl.ds(8 * b, 8), :] = zero
            return carry

        lax.fori_loop(0, cols + 1, one, 0)

        def two(c, carry):
            for k in range(STEPS):
                for i in range(4):
                    fine[k, c, pl.ds(8 * i, 8), :] = zero
            return carry

        lax.fori_loop(0, cols, two, 0)

        def three(c, carry):
            for k in range(STEPS):
                for d in corners:
                    rc[k, d, c] = zero
            return carry

        lax.fori_loop(0, cols // 2 + 1, three, 0)

    def deep(k, slot, first, count, d):
        c = pl.ds(first, count)
        pair = pl.ds(first // 2, (count + 1) // 2)
        if d == UP:
            src, dst = co.at[k, c, pl.ds(4, 3)], co.at[k, c, pl.ds(0, 3)]
        elif d == DOWN:
            src, dst = co.at[k, c, pl.ds(3, 3)], co.at[k, c, pl.ds(7, 3)]
        elif d == RIGHT:
            src, dst = sr.at[c], hl.at[k, c]
        elif d == LEFT:
            src, dst = sl.at[c], hr.at[k, c]
        else:
            src, dst = sc.at[d - 4, pair], rc.at[k, d - 4, pair]
        return pltpu.make_async_remote_copy(
            src_ref=src, dst_ref=dst, send_sem=dsend.at[k, slot, d], recv_sem=drecv.at[k, slot, d],
            device_id=device(*SHIFT[d]), device_id_type=MESH)

    def deep_start(k, slot, first, count):
        for d in (RU, LU, RD, LD, RIGHT, LEFT, UP, DOWN):
            guarded(SHIFT[d][1], lambda d=d: deep(k, slot, first, count, d).start())

    def deep_wait(k, slot, first, count):
        for d in range(8):
            guarded(SHIFT[d][1], lambda d=d: deep(k, slot, first, count, d).wait_send())
            guarded(-SHIFT[d][1], lambda d=d: deep(k, slot, first, count, d).wait_recv())

    half = angs // 2

    def fine_parts(d, part):
        if part is None:
            return pl.ds(0, angs)
        if d == UP:
            return pl.ds(half, half) if part == 0 else pl.ds(0, half)
        if d == DOWN:
            return pl.ds(0, half) if part == 0 else pl.ds(half, half)
        return None if (d == LEFT) != (part == 0) else pl.ds(0, angs)

    def fine(k, g, d, part):
        c = pl.ds(g * per, per)
        rows = fine_parts(d, part)
        if d == UP:
            src, dst = fsu.at[c, rows], fd.at[k, c, rows]
        elif d == DOWN:
            src, dst = fsd.at[c, rows], fu.at[k, c, rows]
        elif d == RIGHT:
            src, dst = vf.at[c, pl.ds(8 * (angs - 1), 8)], fl.at[k, c]
        else:
            src, dst = vf.at[c, pl.ds(0, 8)], fr.at[k, c]
        i = d + 4 if part == 1 else d
        return pltpu.make_async_remote_copy(
            src_ref=src, dst_ref=dst, send_sem=fsend.at[k, g, i], recv_sem=frecv.at[k, g, i],
            device_id=device(*SHIFT[d]), device_id_type=MESH)

    def fine_start(k, g, part):
        for d in (RIGHT, LEFT, UP, DOWN):
            if fine_parts(d, part) is not None:
                guarded(SHIFT[d][1], lambda d=d: fine(k, g, d, part).start())

    def fine_wait(k, g, part):
        for d in range(4):
            if fine_parts(d, part) is not None:
                guarded(SHIFT[d][1], lambda d=d: fine(k, g, d, part).wait_send())
                guarded(-SHIFT[d][1], lambda d=d: fine(k, g, d, part).wait_recv())

    def corner_tiles(k, c):
        low = [co[k, c, 3 + h, pl.ds(0, 8), :] for h in range(4)]
        high = [co[k, c, 3 + h, pl.ds(8, 8), :] for h in range(4)]
        for t in range(2):
            sr[c, pl.ds(8 * t, 8), :] = jnp.where(sub < 4, roll(high[2 * t], 4), high[2 * t + 1])
            sl[c, pl.ds(8 * t, 8), :] = jnp.where(sub < 4, low[2 * t], roll(low[2 * t + 1], 4))
        return (
            jnp.where(sub == 5, roll(high[2], -2), high[3]),
            jnp.where(sub == 2, roll(low[2], 2), low[3]),
            jnp.where(sub == 5, roll(high[1], -2), high[0]),
            jnp.where(sub == 2, roll(low[1], 2), low[0]),
        )

    def merge(d, even, odd):
        if d in (RU, RD):
            return jnp.where(sub < 4, roll(even, 4), odd)
        return jnp.where(sub < 4, even, roll(odd, 4))

    def pack_pair(k, pair):
        even, odd = corner_tiles(k, 2 * pair), corner_tiles(k, 2 * pair + 1)
        for d in (RU, LU, RD, LD):
            sc[d - 4, pair] = merge(d, even[d - 4], odd[d - 4])

    def halo(k, c, pair, parity, h):
        if 0 <= h < 4:
            t = h // 2
            q, p = hr[k, c, pl.ds(8 * t, 8), :], hl[k, c, pl.ds(8 * t, 8), :]
            if h % 2 == 0:
                return jnp.where(sub < 4, q, roll(p, 4))
            return jnp.where(sub < 4, roll(q, 4), p)
        left = rc[k, (RU if h < 0 else RD) - 4, pair]
        right = rc[k, (LU if h < 0 else LD) - 4, pair]
        if parity == 0:
            left = roll(left, 4)
        else:
            right = roll(right, 4)
        if h in (-2, 5):
            left, right = roll(left, 2), roll(right, -2)
        return jnp.where(sub < 4, right, left)

    def ring_row(k, c, pair, parity, h):
        return [co[k, c, 3 + h, pl.ds(0, 8), :], co[k, c, 3 + h, pl.ds(8, 8), :], halo(k, c, pair, parity, h)]

    for copy in in_copies:
        copy.wait()

    def weigh(a, carry):
        rows = pl.ds(pl.multiple_of(a * 8, 8), 8)
        kind = mat[rows, :]
        stiff = zero
        for level in range(modulus.shape[0]):
            stiff = stiff + jnp.where(kind == level, modulus[level], 0.0)
        w = jnp.sqrt(stiff)
        s = sup[rows, :].astype(F32)
        d = SIGMA * w * w + SPRING * s
        weight[rows, :] = w
        spring[rows, :] = s
        diag[rows, :] = d
        kf[rows, :] = OMEGA / d
        return carry

    lax.fori_loop(0, angs, weigh, 0, unroll=4)
    for j in range(4):
        for b in range(2):
            wc = 0.25 * quad(weight, j, b)
            s = 0.25 * quad(spring, j, b)
            kd = OMEGA / (SIGMA * wc * wc + SPRING * s)
            kv[j, pl.ds(8 * b, 8), :] = 0.5 * wc * kd
            iw[j, pl.ds(8 * b, 8), :] = 0.5 / wc
            co[0, pcol, 3 + j, pl.ds(8 * b, 8), :] = wc * wc * kd
    tiles = corner_tiles(0, pcol)
    for d in (RU, LU, RD, LD):
        sc[d - 4, pcol // 2] = merge(d, tiles[d - 4], zero)

    sides = has_up.astype(jnp.int32) + has_down.astype(jnp.int32)
    pl.semaphore_wait(barrier, 2 + 3 * sides)
    tell(0)
    deep_start(0, groups, pcol, 1)

    def restrict(k, c):
        for j in range(4):
            for b in range(2):
                co[k, c, 3 + j, pl.ds(8 * b, 8), :] = kv[j, pl.ds(8 * b, 8), :] * quad(res, j, b, k, c)

    def send_deep(k, g):
        lax.fori_loop(0, per // 2, lambda i, carry: (pack_pair(k, g * (per // 2) + i), carry)[1], 0)
        deep_start(k, g, g * per, per)

    total_angles = na * angs

    def first(g):
        load_copy(g).wait()

        def column(i, carry):
            c = g * per + i
            amount = jnp.where(lax.rem(c, 3) == 2, -LOAD, 0.0)
            spot = jnp.full(T, me_a * angs, jnp.int32) - positions[c // 3]
            for a in range(angs):
                apart = jnp.abs(spot + a)
                near = jnp.minimum(apart, total_angles - apart) < angs
                res[0, c, pl.ds(8 * a, 8), :] += jnp.where(near, amount, 0.0)
            restrict(0, c)
            return carry

        lax.fori_loop(0, per, column, 0)
        send_deep(0, g)

    def coarse_ring():
        deep_wait(0, groups, pcol, 1)
        for h in range(-2, 6):
            row = ring_row(0, pcol, pcol // 2, 0, h)
            for b in range(3):
                pr[h + 2, b] = row[b]

    def sweeps(k, c, pair, parity):
        v0 = {h: ring_row(k, c, pair, parity, h) for h in range(-2, 6)}
        for h in range(-2, 6):
            for b in range(3):
                ring[0, parity, h + 2, b] = v0[h][b]
        outer = {h: [co[k, c, 3 + h, pl.ds(0, 8), :], co[k, c, 3 + h, pl.ds(8, 8), :]] for h in (-3, 6)}
        for sweep in range(3):
            def get(h, b):
                if h in outer:
                    return outer[h][b]
                return ring[sweep, parity, h + 2, b]

            for h in range(-2 + sweep, 6 - sweep):
                edge = h in (-2 + sweep, 5 - sweep)
                me = [get(h, b) for b in range(3)]
                back = [roll(x, 1) for x in me]
                ahead = [roll(x, -1) for x in me]
                for b in range(2 if edge or sweep == 2 else 3):
                    beside = jnp.where(sub == 0, back[b - 1], back[b]) + jnp.where(sub == 7, ahead[(b + 1) % 3], ahead[b])
                    beside = beside + (get(h - 1, b) + get(h + 1, b)) + lanes(me[b])
                    new = (1.0 - OMEGA) * me[b] + ring[0, parity, h + 2, b] + pr[h + 2, b] * beside
                    if sweep < 2:
                        ring[sweep + 1, parity, h + 2, b] = new
                    else:
                        new = new * iw[h, pl.ds(8 * b, 8), :]
                        for da in range(2):
                            for dh in range(2):
                                pe[parity, pl.ds(b * 128 + da * 8 + 2 * h + dh, 8, stride=16), :] = new

    def prolong(k, g, c, parity):
        last = k == STEPS - 1
        acc, square, edges, before = zero, zero, zero, None
        for a in range(angs):
            rows = pl.ds(8 * a, 8)
            r = res[k, c, rows, :]
            z = kf[rows, :] * r + pe[parity, rows, :]
            ys[k, c, rows, :] = z
            acc = acc + r * z
            v = weight[rows, :] * z
            vf[c, rows, :] = v
            if last:
                ahead = jnp.where(sub == 7, 0.0, roll(v, -1)) + jnp.where(lane == 127, 0.0, roll(v, -1, 1))
                square = square + diag[rows, :] * z * z
                edges = edges + v * (ahead if a == 0 else ahead + before)
                before = v
        moments[c, 2 * k] = acc
        if last:
            moments[c, 2 * k + 1] = square - 2.0 * edges - acc
        for i in range(4):
            fsu[c, pl.ds(8 * i, 8), :] = vf[c, pl.ds(64 * i + 7, 8, stride=8), :]
            fsd[c, pl.ds(8 * i, 8), :] = vf[c, pl.ds(64 * i, 8, stride=8), :]

    def precondition(k, g):
        deep_wait(k, g, g * per, per)

        def pair_body(i, carry):
            pair = g * (per // 2) + i
            for parity in range(2):
                sweeps(k, 2 * pair + parity, pair, parity)
            for parity in range(2):
                prolong(k, g, 2 * pair + parity, parity)
            return carry

        lax.fori_loop(0, per // 2, pair_body, 0)
        fine_start(k, g, None if k < STEPS - 1 else 0)

    def apply_fine(k, g):
        fine_wait(k, g, None if k < STEPS - 1 else 1)

        def column(i, carry):
            c = g * per + i
            acc = zero
            before, now = fl[k, c], vf[c, pl.ds(0, 8), :]
            for a in range(angs):
                rows = pl.ds(8 * a, 8)
                after = vf[c, pl.ds(8 * (a + 1), 8), :] if a < angs - 1 else fr[k, c]
                below = jnp.where(sub == 0, fd[k, c, pl.ds(a, 1), :], roll(now, 1))
                above = jnp.where(sub == 7, fu[k, c, pl.ds(a, 1), :], roll(now, -1))
                beside = (before + after) + (below + above) + lanes(now)
                z = ys[k, c, rows, :]
                r = diag[rows, :] * z - weight[rows, :] * beside - res[k, c, rows, :]
                res[k + 1, c, rows, :] = r
                acc = acc + r * z
                before, now = now, after
            if k + 1 < STEPS:
                moments[c, 2 * k + 1] = acc
                restrict(k + 1, c)
            return carry

        lax.fori_loop(0, per, column, 0)
        if k + 1 < STEPS:
            send_deep(k + 1, g)

    def reduce_moments(g):
        for i in range(per):
            c = g * per + i
            rows = zero
            for m in range(2 * STEPS):
                rows = jnp.where(sub == m, jnp.sum(moments[c, m], axis=0, keepdims=True), rows)
            tsum[...] += jnp.where(lane == sub * cols + c, jnp.sum(rows, axis=1, keepdims=True), 0.0)

    def total_moments():
        n, me = na * nh, me_a * nh + me_h
        row[0] = jnp.sum(tsum[...], axis=0, keepdims=True)

        def one(d, carry):
            other = lax.rem(me + d, n)
            pltpu.make_async_remote_copy(
                src_ref=row.at[0], dst_ref=slots.at[me], send_sem=psend, recv_sem=precv,
                device_id={"ang": other // nh, "hgt": lax.rem(other, nh)}, device_id_type=MESH).start()
            return carry

        lax.fori_loop(1, n, one, 0, unroll=True)
        slots[me] = row[0]
        lax.fori_loop(0, groups, lambda g, carry: (apply_fine(STEPS - 1, g), carry)[1], 0)
        many = slots.at[pl.ds(0, n - 1)]
        pltpu.make_async_copy(many, many, psend).wait()
        pltpu.make_async_copy(many, many, precv).wait()
        parts = [slots[i] for i in range(8)]
        for i in range(8, n):
            parts[i % 8] = parts[i % 8] + slots[i]
        while len(parts) > 1:
            parts = [x + y for x, y in zip(parts[::2], parts[1::2])]
        return parts[0]

    def outer_edges(g):
        k = STEPS - 1
        fine_wait(k, g, 0)
        for i in range(per):
            c = g * per + i
            edges = vf[c, pl.ds(8 * (angs - 1), 8), :] * fr[k, c]
            for at in range(0, half, 8):
                low, high = pl.ds(at, 8), pl.ds(half + at, 8)
                edges = edges + fsu[c, low, :] * fu[k, c, low, :] + fsd[c, high, :] * fd[k, c, high, :]
            moments[c, 2 * k + 1] = moments[c, 2 * k + 1] - 2.0 * edges

    def stage(s, g):
        if s == 0:
            first(g)
        elif s % 2:
            precondition(s // 2, g)
        elif s < 2 * STEPS:
            apply_fine(s // 2 - 1, g)
        else:
            outer_edges(g)
            reduce_moments(g)

    tsum[...] = zero
    for t in range(2 * STEPS + 1):
        if t == 1:
            pl.when(jnp.logical_not(has_down))(lambda: clear(0, (RU - 4, LU - 4), fd))
            pl.when(jnp.logical_not(has_up))(lambda: clear(7, (RD - 4, LD - 4), fu))
            coarse_ring()
        lax.fori_loop(0, groups, lambda g, carry: (stage(t, g), carry)[1], 0)
        if t >= 1:
            hear(t - 1)
            tell(t)
        if t == 2 * STEPS - 1:
            lax.fori_loop(0, groups, lambda g, carry: (fine_start(STEPS - 1, g, 1), carry)[1], 0)

    sums[...] = total_moments()


def combine(sums, res, ys, out_x, out_r, coef, xs, rs, sem):
    cols, flat, _ = out_x.shape
    shape = (16, 128)
    sub = lax.broadcasted_iota(jnp.int32, shape, 0)
    lane = lax.broadcasted_iota(jnp.int32, shape, 1)
    m = [jnp.broadcast_to(jnp.sum(jnp.where(lane == sub + i * cols, sums[...], 0.0), axis=1, keepdims=True), shape)
         for i in range(2 * STEPS)]
    none = jnp.zeros(shape, F32)
    one = jnp.ones(shape, F32)
    way, left, made = [one, none, none], [one, none, none, none], [none] * 3
    rz = m[0]
    for k in range(STEPS):
        image = [none] * 4
        for j in range(k + 1):
            image[j + 1] = image[j + 1] + way[j]
            image[j] = image[j] + way[j]
        curve = none
        for i in range(k + 1):
            for j in range(k + 2):
                curve = curve + way[i] * image[j] * m[i + j]
        alpha = rz / curve
        made = [made[j] + alpha * way[j] for j in range(3)]
        left = [left[j] - alpha * image[j] for j in range(4)]
        if k + 1 < STEPS:
            new = none
            for i in range(k + 2):
                for j in range(k + 2):
                    new = new + left[i] * left[j] * m[i + j]
            beta = new / rz
            way = [left[j] + beta * way[j] for j in range(3)]
            rz = new
    for i, x in enumerate(made + left):
        coef[i] = x

    def copies(c):
        return (pltpu.make_async_copy(xs.at[c], out_x.at[c], sem.at[0, c]),
                pltpu.make_async_copy(rs.at[c], out_r.at[c], sem.at[1, c]))

    def column(c, carry):
        x_of = [jnp.broadcast_to(coef[i, pl.ds(c, 1), :], T) for i in range(3)]
        r_of = [jnp.broadcast_to(coef[3 + i, pl.ds(c, 1), :], T) for i in range(4)]
        for a in range(flat // 8):
            rows = pl.ds(8 * a, 8)
            xs[c, rows, :] = x_of[0] * ys[0, c, rows, :] + x_of[1] * ys[1, c, rows, :] + x_of[2] * ys[2, c, rows, :]
            rs[c, rows, :] = (r_of[0] * res[0, c, rows, :] + r_of[1] * res[1, c, rows, :]
                              + r_of[2] * res[2, c, rows, :] + r_of[3] * res[3, c, rows, :])
        for copy in copies(c):
            copy.start()
        return carry

    lax.fori_loop(0, cols, column, 0)
    for c in range(cols):
        for copy in copies(c):
            copy.wait()


def body(loads, material, support, modulus, positions):
    cases, comps, angs, rows, radial = loads.shape
    cols = cases * comps
    na, nh = lax.axis_size("ang"), lax.axis_size("hgt")
    flat = angs * rows
    hbm = pl.BlockSpec(memory_space=pltpu.HBM)
    smem = pl.BlockSpec(memory_space=pltpu.SMEM)
    vmem = pl.BlockSpec(memory_space=pltpu.VMEM)
    v = lambda *shape: pltpu.VMEM((*shape, 128), F32)
    dma = lambda *shape: pltpu.SemaphoreType.DMA(shape)
    res, ys, sums = pl.pallas_call(
        kernel,
        out_shape=(v(STEPS + 1, cols, flat), v(STEPS, cols, flat), v(1)),
        in_specs=[smem, smem, hbm, hbm, hbm],
        out_specs=(vmem, vmem, vmem),
        scratch_shapes=[
            pltpu.VMEM((flat, 128), jnp.int32), pltpu.VMEM((flat, 128), jnp.int32),
            v(flat), v(flat), v(flat), v(flat), v(4, 16), v(4, 16),
            v(cols, flat), v(2, flat),
            v(STEPS, cols + 1, 10, 16),
            v(cols + 1, 16), v(cols + 1, 16), v(4, cols // 2 + 1, 8),
            v(STEPS, cols + 1, 16), v(STEPS, cols + 1, 16), v(STEPS, 4, cols // 2 + 1, 8),
            v(8, 3, 8), v(3, 2, 8, 3, 8),
            v(cols, 32), v(cols, 32), v(STEPS, cols, 32), v(STEPS, cols, 32),
            v(STEPS, cols, 8), v(STEPS, cols, 8),
            v(cols, 2 * STEPS, 8), v(8), v(1, 1), v(na * nh, 1),
            pltpu.SemaphoreType.REGULAR((8,)), dma(GROUPS + 2), dma(STEPS, GROUPS + 1, 8), dma(STEPS, GROUPS + 1, 8),
            dma(STEPS, GROUPS, 8), dma(STEPS, GROUPS, 8), pltpu.SemaphoreType.DMA, pltpu.SemaphoreType.DMA,
        ],
        compiler_params=pltpu.CompilerParams(
            collective_id=0, has_side_effects=True, vmem_limit_bytes=55 * 1000 * 1000),
        name="girder_cg",
    )(modulus, positions, loads.reshape(cols, flat, radial), material.reshape(flat, radial), support.reshape(flat, radial))
    out = jax.ShapeDtypeStruct((cols, flat, radial), F32)
    x, r = pl.pallas_call(
        combine,
        out_shape=(out, out),
        in_specs=[vmem, vmem, vmem],
        out_specs=(hbm, hbm),
        scratch_shapes=[v(2 * STEPS + 1, 16), v(cols, flat), v(cols, flat), dma(2, cols)],
        compiler_params=pltpu.CompilerParams(vmem_limit_bytes=16 * 1024 * 1024),
        name="girder_combine",
    )(sums, res, ys)
    return x.reshape(loads.shape), r.reshape(loads.shape)


def solution(mesh):
    field = P(None, None, "ang", "hgt", None)
    cell = P("ang", "hgt", None)
    return jax.shard_map(body, mesh=mesh, in_specs=(field, cell, cell, P(), P()),
                         out_specs=(field, field), check_vma=False)
```

```python
import functools

import jax
import jax.numpy as jnp
from jax import lax
from jax.experimental import pallas as pl
from jax.experimental.pallas import tpu as pltpu
from jax.sharding import PartitionSpec as P

STEPS = 3
SIGMA = 6.5
SPRING = 20.0
OMEGA = 0.8
LOAD = 3.0
GROUPS = 3
MESH = pl.DeviceIdType.MESH
F32 = jnp.float32
T = (8, 128)
UP, DOWN, RIGHT, LEFT, RU, LU, RD, LD = range(8)
SHIFT = ((0, 1), (0, -1), (1, 0), (-1, 0), (1, 1), (-1, 1), (1, -1), (-1, -1))


def kernel(
    modulus, positions, loads, material, support,
    res, ys, sums,
    mat, sup, weight, spring, diag, kf, kv, iw,
    vf, pe, co, sr, sl, sc, hl, hr, rc, pr, ring,
    fsu, fsd, fu, fd, fl, fr, moments, tsum, row, slots,
    spread, in_sem, dsend, drecv, fsend, frecv, psend, precv,
):
    na, nh = lax.axis_size("ang"), lax.axis_size("hgt")
    me_a, me_h = lax.axis_index("ang"), lax.axis_index("hgt")
    cols = loads.shape[0]
    groups = GROUPS
    per = cols // groups
    pcol = cols
    angs = 32
    sub = lax.broadcasted_iota(jnp.int32, T, 0)
    lane = lax.broadcasted_iota(jnp.int32, T, 1)
    has_up, has_down = me_h < nh - 1, me_h > 0

    def device(da, dh):
        return {"ang": lax.rem(me_a + da + na, na), "hgt": me_h + dh}

    def guarded(dh, body):
        if dh > 0:
            pl.when(has_up)(body)
        elif dh < 0:
            pl.when(has_down)(body)
        else:
            body()

    in_copies = [pltpu.make_async_copy(material, mat, in_sem.at[groups]),
                 pltpu.make_async_copy(support, sup, in_sem.at[groups + 1])]
    for copy in in_copies:
        copy.start()

    def load_copy(g):
        c = pl.ds(g * per, per)
        return pltpu.make_async_copy(loads.at[c], res.at[0, c], in_sem.at[g])

    for g in range(groups):
        load_copy(g).start()

    barrier = pltpu.get_barrier_semaphore()

    def neighbour(da, dh, sem):
        pl.semaphore_signal(sem, inc=1, device_id=device(da, dh), device_id_type=MESH)

    for da, dh in SHIFT:
        guarded(dh, lambda da=da, dh=dh: neighbour(da, dh, barrier))

    rounds = ([(0, 1 << i) for i in range((na // 2 - 1).bit_length())]
              + [(1, 1 << i) for i in range((nh - 1).bit_length())])

    def far(r, body):
        axis, d = rounds[r]
        if axis == 0:
            body(d, 0)
            body(-d, 0)
        else:
            pl.when(me_h + d < nh)(lambda: body(0, d))
            pl.when(me_h - d >= 0)(lambda: body(0, -d))

    def tell(r):
        if r < len(rounds):
            far(r, lambda da, dh: neighbour(da, dh, spread.at[r]))

    def hear(r):
        if r < len(rounds):
            axis, d = rounds[r]
            many = 2 if axis == 0 else (me_h + d < nh).astype(jnp.int32) + (me_h - d >= 0).astype(jnp.int32)
            pl.semaphore_wait(spread.at[r], many)

    def roll(x, shift, axis=0):
        return pltpu.roll(x, shift % x.shape[axis], axis)

    def lanes(v):
        return jnp.where(lane == 0, 0.0, roll(v, 1, 1)) + jnp.where(lane == 127, 0.0, roll(v, -1, 1))

    def quad(ref, j, b, *lead):
        total = None
        for da in range(2):
            for dh in range(2):
                part = ref[(*lead, pl.ds(b * 128 + da * 8 + 2 * j + dh, 8, stride=16), slice(None))]
                total = part if total is None else total + part
        return total

    zero = jnp.zeros(T, F32)

    def clear(row, corners, fine):
        def one(c, carry):
            for k in range(STEPS):
                for j in range(3):
                    for b in range(2):
                        co[k, c, row + j, pl.ds(8 * b, 8), :] = zero
            return carry

        lax.fori_loop(0, cols + 1, one, 0)

        def two(c, carry):
            for k in range(STEPS):
                for i in range(4):
                    fine[k, c, pl.ds(8 * i, 8), :] = zero
            return carry

        lax.fori_loop(0, cols, two, 0)

        def three(c, carry):
            for k in range(STEPS):
                for d in corners:
                    rc[k, d, c] = zero
            return carry

        lax.fori_loop(0, cols // 2 + 1, three, 0)

    def deep(k, slot, first, count, d):
        c = pl.ds(first, count)
        pair = pl.ds(first // 2, (count + 1) // 2)
        if d == UP:
            src, dst = co.at[k, c, pl.ds(4, 3)], co.at[k, c, pl.ds(0, 3)]
        elif d == DOWN:
            src, dst = co.at[k, c, pl.ds(3, 3)], co.at[k, c, pl.ds(7, 3)]
        elif d == RIGHT:
            src, dst = sr.at[c], hl.at[k, c]
        elif d == LEFT:
            src, dst = sl.at[c], hr.at[k, c]
        else:
            src, dst = sc.at[d - 4, pair], rc.at[k, d - 4, pair]
        return pltpu.make_async_remote_copy(
            src_ref=src, dst_ref=dst, send_sem=dsend.at[k, slot, d], recv_sem=drecv.at[k, slot, d],
            device_id=device(*SHIFT[d]), device_id_type=MESH)

    def deep_start(k, slot, first, count):
        for d in (UP, DOWN, RIGHT, LEFT, RU, LU, RD, LD):
            guarded(SHIFT[d][1], lambda d=d: deep(k, slot, first, count, d).start())

    def deep_wait(k, slot, first, count):
        for d in range(8):
            guarded(SHIFT[d][1], lambda d=d: deep(k, slot, first, count, d).wait_send())
            guarded(-SHIFT[d][1], lambda d=d: deep(k, slot, first, count, d).wait_recv())

    half = angs // 2

    def fine_parts(d, part):
        if part is None:
            return pl.ds(0, angs)
        if d == UP:
            return pl.ds(half, half) if part == 0 else pl.ds(0, half)
        if d == DOWN:
            return pl.ds(0, half) if part == 0 else pl.ds(half, half)
        return None if (d == LEFT) != (part == 0) else pl.ds(0, angs)

    def fine(k, g, d, part):
        c = pl.ds(g * per, per)
        rows = fine_parts(d, part)
        if d == UP:
            src, dst = fsu.at[c, rows], fd.at[k, c, rows]
        elif d == DOWN:
            src, dst = fsd.at[c, rows], fu.at[k, c, rows]
        elif d == RIGHT:
            src, dst = vf.at[c, pl.ds(8 * (angs - 1), 8)], fl.at[k, c]
        else:
            src, dst = vf.at[c, pl.ds(0, 8)], fr.at[k, c]
        i = d + 4 if part == 1 else d
        return pltpu.make_async_remote_copy(
            src_ref=src, dst_ref=dst, send_sem=fsend.at[k, g, i], recv_sem=frecv.at[k, g, i],
            device_id=device(*SHIFT[d]), device_id_type=MESH)

    def fine_start(k, g, part):
        for d in (RIGHT, LEFT, UP, DOWN):
            if fine_parts(d, part) is not None:
                guarded(SHIFT[d][1], lambda d=d: fine(k, g, d, part).start())

    def fine_wait(k, g, part):
        for d in range(4):
            if fine_parts(d, part) is not None:
                guarded(SHIFT[d][1], lambda d=d: fine(k, g, d, part).wait_send())
                guarded(-SHIFT[d][1], lambda d=d: fine(k, g, d, part).wait_recv())

    def corner_tiles(k, c):
        low = [co[k, c, 3 + h, pl.ds(0, 8), :] for h in range(4)]
        high = [co[k, c, 3 + h, pl.ds(8, 8), :] for h in range(4)]
        for t in range(2):
            sr[c, pl.ds(8 * t, 8), :] = jnp.where(sub < 4, roll(high[2 * t], 4), high[2 * t + 1])
            sl[c, pl.ds(8 * t, 8), :] = jnp.where(sub < 4, low[2 * t], roll(low[2 * t + 1], 4))
        return (
            jnp.where(sub == 5, roll(high[2], -2), high[3]),
            jnp.where(sub == 2, roll(low[2], 2), low[3]),
            jnp.where(sub == 5, roll(high[1], -2), high[0]),
            jnp.where(sub == 2, roll(low[1], 2), low[0]),
        )

    def merge(d, even, odd):
        if d in (RU, RD):
            return jnp.where(sub < 4, roll(even, 4), odd)
        return jnp.where(sub < 4, even, roll(odd, 4))

    def pack_pair(k, pair):
        even, odd = corner_tiles(k, 2 * pair), corner_tiles(k, 2 * pair + 1)
        for d in (RU, LU, RD, LD):
            sc[d - 4, pair] = merge(d, even[d - 4], odd[d - 4])

    def halo(k, c, pair, parity, h):
        if 0 <= h < 4:
            t = h // 2
            q, p = hr[k, c, pl.ds(8 * t, 8), :], hl[k, c, pl.ds(8 * t, 8), :]
            if h % 2 == 0:
                return jnp.where(sub < 4, q, roll(p, 4))
            return jnp.where(sub < 4, roll(q, 4), p)
        left = rc[k, (RU if h < 0 else RD) - 4, pair]
        right = rc[k, (LU if h < 0 else LD) - 4, pair]
        if parity == 0:
            left = roll(left, 4)
        else:
            right = roll(right, 4)
        if h in (-2, 5):
            left, right = roll(left, 2), roll(right, -2)
        return jnp.where(sub < 4, right, left)

    def ring_row(k, c, pair, parity, h):
        return [co[k, c, 3 + h, pl.ds(0, 8), :], co[k, c, 3 + h, pl.ds(8, 8), :], halo(k, c, pair, parity, h)]

    for copy in in_copies:
        copy.wait()

    def weigh(a, carry):
        rows = pl.ds(pl.multiple_of(a * 8, 8), 8)
        kind = mat[rows, :]
        stiff = zero
        for level in range(modulus.shape[0]):
            stiff = stiff + jnp.where(kind == level, modulus[level], 0.0)
        w = jnp.sqrt(stiff)
        s = sup[rows, :].astype(F32)
        d = SIGMA * w * w + SPRING * s
        weight[rows, :] = w
        spring[rows, :] = s
        diag[rows, :] = d
        kf[rows, :] = OMEGA / d
        return carry

    lax.fori_loop(0, angs, weigh, 0, unroll=4)
    for j in range(4):
        for b in range(2):
            wc = 0.25 * quad(weight, j, b)
            s = 0.25 * quad(spring, j, b)
            kd = OMEGA / (SIGMA * wc * wc + SPRING * s)
            kv[j, pl.ds(8 * b, 8), :] = 0.5 * wc * kd
            iw[j, pl.ds(8 * b, 8), :] = 0.5 / wc
            co[0, pcol, 3 + j, pl.ds(8 * b, 8), :] = wc * wc * kd
    tiles = corner_tiles(0, pcol)
    for d in (RU, LU, RD, LD):
        sc[d - 4, pcol // 2] = merge(d, tiles[d - 4], zero)

    sides = has_up.astype(jnp.int32) + has_down.astype(jnp.int32)
    pl.semaphore_wait(barrier, 2 + 3 * sides)
    tell(0)
    deep_start(0, groups, pcol, 1)

    def restrict(k, c):
        for j in range(4):
            for b in range(2):
                co[k, c, 3 + j, pl.ds(8 * b, 8), :] = kv[j, pl.ds(8 * b, 8), :] * quad(res, j, b, k, c)

    def send_deep(k, g):
        lax.fori_loop(0, per // 2, lambda i, carry: (pack_pair(k, g * (per // 2) + i), carry)[1], 0)
        deep_start(k, g, g * per, per)

    total_angles = na * angs

    def first(g):
        load_copy(g).wait()

        def column(i, carry):
            c = g * per + i
            amount = jnp.where(lax.rem(c, 3) == 2, -LOAD, 0.0)
            spot = jnp.full(T, me_a * angs, jnp.int32) - positions[c // 3]
            for a in range(angs):
                apart = jnp.abs(spot + a)
                near = jnp.minimum(apart, total_angles - apart) < angs
                res[0, c, pl.ds(8 * a, 8), :] += jnp.where(near, amount, 0.0)
            restrict(0, c)
            return carry

        lax.fori_loop(0, per, column, 0)
        send_deep(0, g)

    def coarse_ring():
        deep_wait(0, groups, pcol, 1)
        for h in range(-2, 6):
            row = ring_row(0, pcol, pcol // 2, 0, h)
            for b in range(3):
                pr[h + 2, b] = row[b]

    def sweeps(k, c, pair, parity):
        v0 = {h: ring_row(k, c, pair, parity, h) for h in range(-2, 6)}
        for h in range(-2, 6):
            for b in range(3):
                ring[0, parity, h + 2, b] = v0[h][b]
        outer = {h: [co[k, c, 3 + h, pl.ds(0, 8), :], co[k, c, 3 + h, pl.ds(8, 8), :]] for h in (-3, 6)}
        for sweep in range(3):
            def get(h, b):
                if h in outer:
                    return outer[h][b]
                return ring[sweep, parity, h + 2, b]

            for h in range(-2 + sweep, 6 - sweep):
                edge = h in (-2 + sweep, 5 - sweep)
                me = [get(h, b) for b in range(3)]
                back = [roll(x, 1) for x in me]
                ahead = [roll(x, -1) for x in me]
                for b in range(2 if edge or sweep == 2 else 3):
                    beside = jnp.where(sub == 0, back[b - 1], back[b]) + jnp.where(sub == 7, ahead[(b + 1) % 3], ahead[b])
                    beside = beside + (get(h - 1, b) + get(h + 1, b)) + lanes(me[b])
                    new = (1.0 - OMEGA) * me[b] + ring[0, parity, h + 2, b] + pr[h + 2, b] * beside
                    if sweep < 2:
                        ring[sweep + 1, parity, h + 2, b] = new
                    else:
                        new = new * iw[h, pl.ds(8 * b, 8), :]
                        for da in range(2):
                            for dh in range(2):
                                pe[parity, pl.ds(b * 128 + da * 8 + 2 * h + dh, 8, stride=16), :] = new

    def prolong(k, g, c, parity):
        last = k == STEPS - 1
        acc, square, edges, before = zero, zero, zero, None
        for a in range(angs):
            rows = pl.ds(8 * a, 8)
            r = res[k, c, rows, :]
            z = kf[rows, :] * r + pe[parity, rows, :]
            ys[k, c, rows, :] = z
            acc = acc + r * z
            v = weight[rows, :] * z
            vf[c, rows, :] = v
            if last:
                ahead = jnp.where(sub == 7, 0.0, roll(v, -1)) + jnp.where(lane == 127, 0.0, roll(v, -1, 1))
                square = square + diag[rows, :] * z * z
                edges = edges + v * (ahead if a == 0 else ahead + before)
                before = v
        moments[c, 2 * k] = acc
        if last:
            moments[c, 2 * k + 1] = square - 2.0 * edges - acc
        for i in range(4):
            fsu[c, pl.ds(8 * i, 8), :] = vf[c, pl.ds(64 * i + 7, 8, stride=8), :]
            fsd[c, pl.ds(8 * i, 8), :] = vf[c, pl.ds(64 * i, 8, stride=8), :]

    def precondition(k, g):
        deep_wait(k, g, g * per, per)

        def pair_body(i, carry):
            pair = g * (per // 2) + i
            for parity in range(2):
                sweeps(k, 2 * pair + parity, pair, parity)
            for parity in range(2):
                prolong(k, g, 2 * pair + parity, parity)
            return carry

        lax.fori_loop(0, per // 2, pair_body, 0)
        fine_start(k, g, None if k < STEPS - 1 else 0)

    def apply_fine(k, g):
        fine_wait(k, g, None if k < STEPS - 1 else 1)

        def column(i, carry):
            c = g * per + i
            acc = zero
            before, now = fl[k, c], vf[c, pl.ds(0, 8), :]
            for a in range(angs):
                rows = pl.ds(8 * a, 8)
                after = vf[c, pl.ds(8 * (a + 1), 8), :] if a < angs - 1 else fr[k, c]
                below = jnp.where(sub == 0, fd[k, c, pl.ds(a, 1), :], roll(now, 1))
                above = jnp.where(sub == 7, fu[k, c, pl.ds(a, 1), :], roll(now, -1))
                beside = (before + after) + (below + above) + lanes(now)
                z = ys[k, c, rows, :]
                r = diag[rows, :] * z - weight[rows, :] * beside - res[k, c, rows, :]
                res[k + 1, c, rows, :] = r
                acc = acc + r * z
                before, now = now, after
            if k + 1 < STEPS:
                moments[c, 2 * k + 1] = acc
                restrict(k + 1, c)
            return carry

        lax.fori_loop(0, per, column, 0)
        if k + 1 < STEPS:
            send_deep(k + 1, g)

    def reduce_moments(g):
        for i in range(per):
            c = g * per + i
            rows = zero
            for m in range(2 * STEPS):
                rows = jnp.where(sub == m, jnp.sum(moments[c, m], axis=0, keepdims=True), rows)
            tsum[...] += jnp.where(lane == sub * cols + c, jnp.sum(rows, axis=1, keepdims=True), 0.0)

    def total_moments():
        n, me = na * nh, me_a * nh + me_h
        row[0] = jnp.sum(tsum[...], axis=0, keepdims=True)

        def one(d, carry):
            other = lax.rem(me + d, n)
            pltpu.make_async_remote_copy(
                src_ref=row.at[0], dst_ref=slots.at[me], send_sem=psend, recv_sem=precv,
                device_id={"ang": other // nh, "hgt": lax.rem(other, nh)}, device_id_type=MESH).start()
            return carry

        lax.fori_loop(1, n, one, 0, unroll=True)
        slots[me] = row[0]
        lax.fori_loop(0, groups, lambda g, carry: (apply_fine(STEPS - 1, g), carry)[1], 0)
        many = slots.at[pl.ds(0, n - 1)]
        pltpu.make_async_copy(many, many, psend).wait()
        pltpu.make_async_copy(many, many, precv).wait()
        parts = [slots[i] for i in range(8)]
        for i in range(8, n):
            parts[i % 8] = parts[i % 8] + slots[i]
        while len(parts) > 1:
            parts = [x + y for x, y in zip(parts[::2], parts[1::2])]
        return parts[0]

    def outer_edges(g):
        k = STEPS - 1
        fine_wait(k, g, 0)
        for i in range(per):
            c = g * per + i
            edges = vf[c, pl.ds(8 * (angs - 1), 8), :] * fr[k, c]
            for at in range(0, half, 8):
                low, high = pl.ds(at, 8), pl.ds(half + at, 8)
                edges = edges + fsu[c, low, :] * fu[k, c, low, :] + fsd[c, high, :] * fd[k, c, high, :]
            moments[c, 2 * k + 1] = moments[c, 2 * k + 1] - 2.0 * edges

    def stage(s, g):
        if s == 0:
            first(g)
        elif s % 2:
            precondition(s // 2, g)
        elif s < 2 * STEPS:
            apply_fine(s // 2 - 1, g)
        else:
            outer_edges(g)
            reduce_moments(g)

    tsum[...] = zero
    for t in range(2 * STEPS + 1):
        if t == 1:
            pl.when(jnp.logical_not(has_down))(lambda: clear(0, (RU - 4, LU - 4), fd))
            pl.when(jnp.logical_not(has_up))(lambda: clear(7, (RD - 4, LD - 4), fu))
            coarse_ring()
        lax.fori_loop(0, groups, lambda g, carry: (stage(t, g), carry)[1], 0)
        if t >= 1:
            hear(t - 1)
            tell(t)
        if t == 2 * STEPS - 1:
            lax.fori_loop(0, groups, lambda g, carry: (fine_start(STEPS - 1, g, 1), carry)[1], 0)

    sums[...] = total_moments()


def combine(sums, res, ys, out_x, out_r, coef, xs, rs, sem):
    cols, flat, _ = out_x.shape
    shape = (16, 128)
    sub = lax.broadcasted_iota(jnp.int32, shape, 0)
    lane = lax.broadcasted_iota(jnp.int32, shape, 1)
    m = [jnp.broadcast_to(jnp.sum(jnp.where(lane == sub + i * cols, sums[...], 0.0), axis=1, keepdims=True), shape)
         for i in range(2 * STEPS)]
    none = jnp.zeros(shape, F32)
    one = jnp.ones(shape, F32)
    way, left, made = [one, none, none], [one, none, none, none], [none] * 3
    rz = m[0]
    for k in range(STEPS):
        image = [none] * 4
        for j in range(k + 1):
            image[j + 1] = image[j + 1] + way[j]
            image[j] = image[j] + way[j]
        curve = none
        for i in range(k + 1):
            for j in range(k + 2):
                curve = curve + way[i] * image[j] * m[i + j]
        alpha = rz / curve
        made = [made[j] + alpha * way[j] for j in range(3)]
        left = [left[j] - alpha * image[j] for j in range(4)]
        if k + 1 < STEPS:
            new = none
            for i in range(k + 2):
                for j in range(k + 2):
                    new = new + left[i] * left[j] * m[i + j]
            beta = new / rz
            way = [left[j] + beta * way[j] for j in range(3)]
            rz = new
    for i, x in enumerate(made + left):
        coef[i] = x

    def copies(c):
        return (pltpu.make_async_copy(xs.at[c], out_x.at[c], sem.at[0, c]),
                pltpu.make_async_copy(rs.at[c], out_r.at[c], sem.at[1, c]))

    def column(c, carry):
        x_of = [jnp.broadcast_to(coef[i, pl.ds(c, 1), :], T) for i in range(3)]
        r_of = [jnp.broadcast_to(coef[3 + i, pl.ds(c, 1), :], T) for i in range(4)]
        for a in range(flat // 8):
            rows = pl.ds(8 * a, 8)
            xs[c, rows, :] = x_of[0] * ys[0, c, rows, :] + x_of[1] * ys[1, c, rows, :] + x_of[2] * ys[2, c, rows, :]
            rs[c, rows, :] = (r_of[0] * res[0, c, rows, :] + r_of[1] * res[1, c, rows, :]
                              + r_of[2] * res[2, c, rows, :] + r_of[3] * res[3, c, rows, :])
        for copy in copies(c):
            copy.start()
        return carry

    lax.fori_loop(0, cols, column, 0)
    for c in range(cols):
        for copy in copies(c):
            copy.wait()


def body(loads, material, support, modulus, positions):
    cases, comps, angs, rows, radial = loads.shape
    cols = cases * comps
    na, nh = lax.axis_size("ang"), lax.axis_size("hgt")
    flat = angs * rows
    hbm = pl.BlockSpec(memory_space=pltpu.HBM)
    smem = pl.BlockSpec(memory_space=pltpu.SMEM)
    vmem = pl.BlockSpec(memory_space=pltpu.VMEM)
    v = lambda *shape: pltpu.VMEM((*shape, 128), F32)
    dma = lambda *shape: pltpu.SemaphoreType.DMA(shape)
    res, ys, sums = pl.pallas_call(
        kernel,
        out_shape=(v(STEPS + 1, cols, flat), v(STEPS, cols, flat), v(1)),
        in_specs=[smem, smem, hbm, hbm, hbm],
        out_specs=(vmem, vmem, vmem),
        scratch_shapes=[
            pltpu.VMEM((flat, 128), jnp.int32), pltpu.VMEM((flat, 128), jnp.int32),
            v(flat), v(flat), v(flat), v(flat), v(4, 16), v(4, 16),
            v(cols, flat), v(2, flat),
            v(STEPS, cols + 1, 10, 16),
            v(cols + 1, 16), v(cols + 1, 16), v(4, cols // 2 + 1, 8),
            v(STEPS, cols + 1, 16), v(STEPS, cols + 1, 16), v(STEPS, 4, cols // 2 + 1, 8),
            v(8, 3, 8), v(3, 2, 8, 3, 8),
            v(cols, 32), v(cols, 32), v(STEPS, cols, 32), v(STEPS, cols, 32),
            v(STEPS, cols, 8), v(STEPS, cols, 8),
            v(cols, 2 * STEPS, 8), v(8), v(1, 1), v(na * nh, 1),
            pltpu.SemaphoreType.REGULAR((8,)), dma(GROUPS + 2), dma(STEPS, GROUPS + 1, 8), dma(STEPS, GROUPS + 1, 8),
            dma(STEPS, GROUPS, 8), dma(STEPS, GROUPS, 8), pltpu.SemaphoreType.DMA, pltpu.SemaphoreType.DMA,
        ],
        compiler_params=pltpu.CompilerParams(
            collective_id=0, has_side_effects=True, vmem_limit_bytes=55 * 1000 * 1000),
        name="girder_cg",
    )(modulus, positions, loads.reshape(cols, flat, radial), material.reshape(flat, radial), support.reshape(flat, radial))
    out = jax.ShapeDtypeStruct((cols, flat, radial), F32)
    x, r = pl.pallas_call(
        combine,
        out_shape=(out, out),
        in_specs=[vmem, vmem, vmem],
        out_specs=(hbm, hbm),
        scratch_shapes=[v(2 * STEPS + 1, 16), v(cols, flat), v(cols, flat), dma(2, cols)],
        compiler_params=pltpu.CompilerParams(vmem_limit_bytes=16 * 1024 * 1024),
        name="girder_combine",
    )(sums, res, ys)
    return x.reshape(loads.shape), r.reshape(loads.shape)


def solution(mesh):
    field = P(None, None, "ang", "hgt", None)
    cell = P("ang", "hgt", None)
    return jax.shard_map(body, mesh=mesh, in_specs=(field, cell, cell, P(), P()),
                         out_specs=(field, field), check_vma=False)
```
